512 devices in a mesh: group: 8 (over y, x_lo), expert: 64 (over z, x_hi, core).
Axes of the slice: x: 4 (x_hi: 2, x_lo: 2; x = x_hi * 2 + x_lo), y: 4, z: 16, core: 2. Of those that a mesh axis runs over, the one named last changes fastest.
Arguments:
- inputs: bfloat16 [3, 4096, 2048], P(None, ('group', 'expert')), may hold values from -6 to 6
- queries: bfloat16 [3, 4096, 2048], P(None, ('group', 'expert')), may hold values from -24 to 24
- new_keys: bfloat16 [3, 4096, 128], P(None, ('group', 'expert')), may hold values from -8 to 8
- new_values: bfloat16 [3, 4096, 128], P(None, ('group', 'expert')), may hold values from -6 to 6
- key_cache: bfloat16 [4096, 384, 128], P(('group', 'expert')), may hold values from -4.5 to 4.5
- value_cache: bfloat16 [4096, 384, 128], P(('group', 'expert')), may hold values from -6 to 6
- cache_lengths: int32 [4096], P(('group', 'expert')), may hold values from 48 to 384, as said below
- expert_ids: int32 [3, 4096, 8], P(None, ('group', 'expert')), may hold values from 0 to 63, all different within a row; in each aligned block of 8 rows (0 to 7, 8 to 15, ..., all dimensions but the last counted through in order) at most 2 rows name the same one
- route_weights: float32 [3, 4096, 8], P(None, ('group', 'expert')), may hold values from 0.03 to 0.5
- w_gate: bfloat16 [64, 2048, 768], P('expert', 'group'), may hold values from -0.125 to 0.125
- w_up: bfloat16 [64, 2048, 768], P('expert', 'group'), may hold values from -0.125 to 0.125
- w_down: bfloat16 [64, 768, 2048], P('expert', None, 'group'), may hold values from -0.21875 to 0.21875
Outputs:
- layer_out: bfloat16 [3, 4096, 2048], P(None, ('group', 'expert'))
The draws below stay inside these ranges and needn't reach their ends.
Inputs may be any that keep to these rules, and one draw needn't show every extreme that they name: `expert_ids`: in each step, no expert is named by more than 2 of the 8 rows of one aligned block. `cache_lengths`: in each aligned block of 8 rows one row has all 384 positions valid.
All inputs are finite; a program needn't handle non-finite values.
Results may differ from the reference program's by a relative error of at most 0.014.
Values may be sent and summed in bfloat16 or wider, within the bound.
No kernel may reach another device: no remote copies, remote signals or barrier semaphores. Data moves between devices by JAX's collectives and lax.ppermute only.
A program may use at most 64 MiB of HBM per device.

```python
import math
import jax
import jax.numpy as jnp
import numpy as np
from jax import lax

D = 2048
FF = 768
HEADS = 32
KV_HEADS = 2
HEAD_DIM = 64
TOPK = 8
CACHE = 384
STEPS = 3
ROWS_DEV = 8
EXPERTS = 64
ROWS = 4096
CAP = 2


def drawn(key):
    base_key = jax.random.fold_in(key, 7)
    key_cache_draw, key_query = jax.random.split(base_key, 2)
    feature_dim = KV_HEADS * HEAD_DIM
    cache_vals = jnp.clip(jax.random.normal(key_cache_draw, (ROWS, CACHE, feature_dim), jnp.float32), -4.5, 4.5)
    query_vals = jnp.clip(jax.random.normal(key_query, (STEPS, ROWS, HEADS * HEAD_DIM), jnp.float32), -4.5, 4.5)
    return (cache_vals, query_vals)


def draw_key_cache(key, part):
    return drawn(key)[0].astype(jnp.bfloat16)


def draw_queries(key, part):
    return drawn(key)[1].astype(jnp.bfloat16)


def draw_cache_lengths(key, part):
    key_one, key_two = jax.random.split(jax.random.fold_in(key, 3))
    lengths = jax.random.randint(key_one, (ROWS,), CACHE // 8, CACHE + 1)
    full_row = jax.random.randint(key_two, (ROWS // ROWS_DEV,), 0, ROWS_DEV)
    inside = jnp.arange(ROWS) % ROWS_DEV
    return jnp.where(inside == jnp.repeat(full_row, ROWS_DEV), CACHE, lengths).astype(jnp.int32)


def block_levels(stream_key, dims, cuts, smallest, largest):
    factor_of = 1.0
    for dim, shards_of in cuts:
        draws = jax.random.uniform(jax.random.fold_in(jax.random.fold_in(stream_key, 6), dim), (shards_of,), jnp.float32, smallest / len(cuts), largest / len(cuts))
        factor_of = factor_of * jnp.repeat(jnp.exp(draws), dims[dim] // shards_of).reshape((-1,) + (1,) * (len(dims) - 1 - dim))
    return factor_of


def deal_out(key, own, number, rows, amount, top, reach, lean):
    ranking = jax.random.permutation(key, amount)
    heavy_load, common = load_shares(amount, rows * top, reach, lean, True), load_shares(amount, rows * top, reach, lean, False)
    places = jnp.arange(amount)

    def named(sizes, rotation):
        used = int((sizes > 0).sum())
        fixed = max(1, used // 4)
        passed = fixed + (places - fixed + rotation * (used - fixed)) % max(1, amount - fixed)
        return jnp.zeros((amount,), jnp.int32).at[ranking[jnp.where(places < fixed, places, passed)]].set(jnp.asarray(sizes, jnp.int32))

    sizes = jnp.where(number % 4 == 0, named(heavy_load, number // 4), named(common, number - number // 4 - 1))
    mixed = jax.random.permutation(jax.random.fold_in(own, 3), amount)
    giver, taker = mixed[0:amount // 2 * 2:2], mixed[1:amount // 2 * 2:2]
    margin = jnp.minimum(sizes[giver] - 1, reach - sizes[taker]) // 2
    margin = jnp.where((giver == ranking[0]) | (taker == ranking[0]) | (sizes[taker] == 0), 0, jnp.maximum(margin, 0))
    passed = jax.random.randint(jax.random.fold_in(own, 4), (amount // 2,), 0, 1 << 20) % (margin + 1)
    sizes = sizes.at[giver].add(-passed).at[taker].add(passed)
    items = jnp.searchsorted(jnp.cumsum(sizes), jnp.arange(rows * top), side="right").astype(jnp.int32)
    listing = items.reshape(top, rows).T
    listing = listing[jax.random.permutation(jax.random.fold_in(own, 1), rows)]
    rotation = jax.random.randint(jax.random.fold_in(own, 2), (rows, 1), 0, top)
    return jnp.take_along_axis(listing, (jnp.arange(top)[None, :] + rotation) % top, axis=1)


def load_shares(amount, total, bound, lean, full):
    loads = [(1 << 20) // math.isqrt(rank ** lean) + 1 for rank in range(1, amount + 1)]
    largest = bound if full else min(bound, max(-(-total // amount), total * loads[0] // sum(loads)))
    least = 1 if total - largest >= amount - 1 else 0
    holding, surplus = [largest] + [least] * (amount - 1), total - largest - least * (amount - 1)
    while surplus > 0:
        candidates = [i for i in range(1, amount) if holding[i] < largest] or [i for i in range(1, amount) if holding[i] < bound]
        mass, left = sum([loads[i] for i in candidates]), surplus
        for i in candidates:
            addition = min(bound - holding[i], max(1, left * loads[i] // mass), surplus)
            holding[i] = holding[i] + addition
            surplus = surplus - addition
    return np.array(holding)


def bell_draw(rng, dims, scale, bound, cuts=(), kind=jnp.bfloat16):
    array = scale * jax.random.normal(rng, dims, jnp.float32)
    if cuts:
        array = array * block_levels(rng, dims, cuts, -0.22, 0.18)
    return jnp.clip(array, -bound, bound).astype(kind)


def setup_inputs(seed: int = 0) -> dict:
    key_list = jax.random.split(jax.random.key(seed), 13)
    inputs = bell_draw(key_list[0], (STEPS, ROWS, D), 1.0, 6.0, ((1, 512),))
    queries = draw_queries(jax.random.fold_in(key_list[12], 71), 0)
    new_keys = bell_draw(key_list[2], (STEPS, ROWS, KV_HEADS * HEAD_DIM), 2.0, 8.0, ((1, 512),))
    new_values = bell_draw(key_list[3], (STEPS, ROWS, KV_HEADS * HEAD_DIM), 1.0, 6.0, ((1, 512),))
    key_cache = draw_key_cache(jax.random.fold_in(key_list[12], 71), 0)
    value_cache = bell_draw(key_list[5], (ROWS, CACHE, KV_HEADS * HEAD_DIM), 1.0, 6.0, ((0, 512),))
    cache_lengths = draw_cache_lengths(jax.random.fold_in(key_list[12], 71), 0)
    expert_ids_keys = jax.random.split(jax.random.fold_in(key_list[7], 1), STEPS * ROWS // ROWS_DEV)
    expert_ids_turns = jax.random.permutation(jax.random.fold_in(key_list[7], 3), STEPS * ROWS // ROWS_DEV)
    expert_ids = jax.vmap(lambda own, number: deal_out(jax.random.fold_in(key_list[7], 2), own, number, ROWS_DEV, EXPERTS, TOPK, CAP, 2))(expert_ids_keys, expert_ids_turns).reshape((STEPS, ROWS, TOPK))
    route_weights = jnp.clip(jnp.exp(math.log(0.5) - 2.8134107 * jax.random.uniform(key_list[8], (STEPS, ROWS, TOPK), jnp.float32) ** block_levels(key_list[8], (STEPS, ROWS, TOPK), ((1, 512),), -0.2, 0.2)), 0.03, 0.5)
    w_gate = bell_draw(key_list[9], (EXPERTS, D, FF), D ** -0.5, 0.125, ((0, 64), (1, 8)))
    w_up = bell_draw(key_list[10], (EXPERTS, D, FF), D ** -0.5, 0.125, ((0, 64), (1, 8)))
    w_down = bell_draw(key_list[11], (EXPERTS, FF, D), FF ** -0.5, 0.21875, ((0, 64), (2, 8)))
    return dict(inputs=inputs, queries=queries, new_keys=new_keys, new_values=new_values, key_cache=key_cache, value_cache=value_cache, cache_lengths=cache_lengths, expert_ids=expert_ids, route_weights=route_weights, w_gate=w_gate, w_up=w_up, w_down=w_down)


def attend_block(query_vals, key_rows, value_rows, valid_mask):
    scores = jnp.einsum("bkgd,bjkd->bkgj", query_vals, key_rows) * (HEAD_DIM ** -0.5)
    scores = jnp.where(valid_mask[:, None, None, :], scores, -1e30)
    highest = jnp.max(scores, axis=-1, keepdims=True)
    weights = jnp.exp(scores - highest)
    probs = (weights / jnp.sum(weights, axis=-1, keepdims=True)).astype(jnp.bfloat16)
    return jnp.einsum("bkgj,bjkd->bkgd", probs.astype(jnp.float32), value_rows)


def reference(inputs, queries, new_keys, new_values, key_cache, value_cache, cache_lengths, expert_ids, route_weights, w_gate, w_up, w_down):
    per_group = HEADS // KV_HEADS
    row_block = math.gcd(ROWS, 512)
    num_blocks = ROWS // row_block
    limit = CAP * (ROWS // ROWS_DEV)
    results = []
    for step_index in range(STEPS):
        fresh = step_index + 1

        def one_block(pieces):
            query_b, key_b, value_b, fresh_k, fresh_v, length_b = pieces
            key_rows = jnp.concatenate([key_b, fresh_k], axis=1).astype(jnp.float32).reshape(row_block, CACHE + fresh, KV_HEADS, HEAD_DIM)
            value_rows = jnp.concatenate([value_b, fresh_v], axis=1).astype(jnp.float32).reshape(row_block, CACHE + fresh, KV_HEADS, HEAD_DIM)
            cache_ok = jnp.arange(CACHE, dtype=jnp.int32)[None, :] < length_b[:, None]
            valid_mask = jnp.concatenate([cache_ok, jnp.ones((row_block, fresh), dtype=bool)], axis=1)
            query_vals = query_b.astype(jnp.float32).reshape(row_block, KV_HEADS, per_group, HEAD_DIM)
            return attend_block(query_vals, key_rows, value_rows, valid_mask).reshape(row_block, D)

        attended = lax.map(one_block, (
            queries[step_index].reshape(num_blocks, row_block, D),
            key_cache.reshape(num_blocks, row_block, CACHE, KV_HEADS * HEAD_DIM),
            value_cache.reshape(num_blocks, row_block, CACHE, KV_HEADS * HEAD_DIM),
            jnp.swapaxes(new_keys[:fresh], 0, 1).reshape(num_blocks, row_block, fresh, KV_HEADS * HEAD_DIM),
            jnp.swapaxes(new_values[:fresh], 0, 1).reshape(num_blocks, row_block, fresh, KV_HEADS * HEAD_DIM),
            cache_lengths.reshape(num_blocks, row_block))).reshape(ROWS, D)
        hidden = (inputs[step_index].astype(jnp.float32) + attended).astype(jnp.bfloat16)
        flat_ids = expert_ids[step_index].reshape(-1)
        flat_weights = route_weights[step_index].reshape(-1)

        def one_expert(running, expert):
            matches = flat_ids == expert
            picked_at = jnp.nonzero(matches, size=limit, fill_value=0)[0].astype(jnp.int32)
            is_used = jnp.arange(limit, dtype=jnp.int32) < jnp.sum(matches.astype(jnp.int32))
            row_index = (picked_at // TOPK).astype(jnp.int32)
            tokens = hidden[row_index].astype(jnp.float32)
            gate_val = jnp.dot(tokens, w_gate[expert].astype(jnp.float32), precision=lax.Precision.HIGHEST)
            up_val = jnp.dot(tokens, w_up[expert].astype(jnp.float32), precision=lax.Precision.HIGHEST)
            activated = (jax.nn.silu(gate_val) * up_val).astype(jnp.bfloat16)
            expert_out = jnp.dot(activated.astype(jnp.float32), w_down[expert].astype(jnp.float32), precision=lax.Precision.HIGHEST).astype(jnp.bfloat16)
            factor = jnp.where(is_used, flat_weights[picked_at], jnp.zeros((), jnp.float32))
            return running.at[row_index].add(factor[:, None] * expert_out.astype(jnp.float32)), None

        running, _ = lax.scan(one_expert, jnp.zeros((ROWS, D), jnp.float32), jnp.arange(EXPERTS, dtype=jnp.int32))
        results.append((hidden.astype(jnp.float32) + running).astype(jnp.bfloat16))
    return jnp.stack(results)
```

```python
import jax
import jax.numpy as jnp
from jax import lax
from jax.sharding import PartitionSpec as P

HEADS = 32
KV_HEADS = 2
HEAD_DIM = 64
TOPK = 8
CACHE = 384
STEPS = 3


def attend_rows(query_vals, key_rows, value_rows, cache_ok, fresh_keys, fresh_values):
    factor = HEAD_DIM ** (-0.5)
    old_scores = (
        jnp.einsum("bkgd,bjkd->bkgj", query_vals, key_rows, preferred_element_type=jnp.float32)
        * factor
    )
    old_scores = jnp.where(cache_ok[:, None, None, :], old_scores, -1e30)
    new_scores = (
        jnp.einsum("bkgd,bjkd->bkgj", query_vals, fresh_keys, preferred_element_type=jnp.float32)
        * factor
    )
    highest = jnp.maximum(
        jnp.max(old_scores, axis=-1, keepdims=True), jnp.max(new_scores, axis=-1, keepdims=True)
    )
    old_weights = jnp.exp(old_scores - highest)
    new_weights = jnp.exp(new_scores - highest)
    denom_sum = jnp.sum(old_weights, axis=-1, keepdims=True) + jnp.sum(
        new_weights, axis=-1, keepdims=True
    )
    old_probs = (old_weights / denom_sum).astype(jnp.bfloat16)
    new_probs = (new_weights / denom_sum).astype(jnp.bfloat16)
    attended = jnp.einsum(
        "bkgj,bjkd->bkgd", old_probs, value_rows, preferred_element_type=jnp.float32
    )
    return attended + jnp.einsum(
        "bkgj,bjkd->bkgd", new_probs, fresh_values, preferred_element_type=jnp.float32
    )


def shards(
    inputs,
    queries,
    new_keys,
    new_values,
    key_cache,
    value_cache,
    cache_lengths,
    expert_ids,
    route_weights,
    w_gate,
    w_up,
    w_down,
):
    experts_all = lax.axis_size("expert")
    rows_dev = inputs.shape[1]
    per_group = HEADS // KV_HEADS
    capacity = max(2, 2 * rows_dev * TOPK // experts_all)
    shares = lax.axis_size("group")

    def gather_shares(weight):
        copies = jnp.broadcast_to(weight, (shares,) + weight.shape[1:])
        return lax.all_to_all(copies, "group", split_axis=0, concat_axis=0, tiled=True)

    gate_mat = gather_shares(w_gate).reshape(-1, w_gate.shape[2])
    up_mat = gather_shares(w_up).reshape(-1, w_up.shape[2])
    down_blocks = gather_shares(w_down)
    key_rows = key_cache.reshape(rows_dev, CACHE, KV_HEADS, HEAD_DIM)
    value_rows = value_cache.reshape(rows_dev, CACHE, KV_HEADS, HEAD_DIM)
    cache_ok = jnp.arange(CACHE, dtype=jnp.int32)[None, :] < cache_lengths[:, None]
    slot_columns = jnp.arange(experts_all * capacity, dtype=jnp.int32)
    expert_range = jnp.arange(experts_all, dtype=jnp.int32)
    results = []
    for step_index in range(STEPS):
        fresh = step_index + 1
        fresh_keys = jnp.swapaxes(new_keys[:fresh], 0, 1).reshape(
            rows_dev, fresh, KV_HEADS, HEAD_DIM
        )
        fresh_values = jnp.swapaxes(new_values[:fresh], 0, 1).reshape(
            rows_dev, fresh, KV_HEADS, HEAD_DIM
        )
        query_vals = queries[step_index].reshape(rows_dev, KV_HEADS, per_group, HEAD_DIM)
        attended = attend_rows(query_vals, key_rows, value_rows, cache_ok, fresh_keys, fresh_values)
        hidden = (inputs[step_index].astype(jnp.float32) + attended.reshape(rows_dev, -1)).astype(
            jnp.bfloat16
        )
        chosen = expert_ids[step_index].reshape(-1)
        onehot = (chosen[:, None] == expert_range[None, :]).astype(jnp.int32)
        before = jnp.cumsum(onehot, axis=0) - onehot
        slot_rank = jnp.sum(before * onehot, axis=1)
        target = chosen * capacity + slot_rank
        placed = (target[:, None] == slot_columns[None, :]).reshape(rows_dev, TOPK, -1)
        spread = jnp.any(placed, axis=1).astype(jnp.bfloat16)
        outgoing = jnp.einsum(
            "rc,rd->cd", spread, hidden, preferred_element_type=jnp.float32
        ).astype(jnp.bfloat16)
        outgoing = outgoing.reshape(experts_all, capacity, -1)
        mixing = jnp.sum(jnp.where(placed, route_weights[step_index][:, :, None], 0.0), axis=1)
        arrived = lax.all_to_all(outgoing, "expert", split_axis=0, concat_axis=0, tiled=True)
        num_slots, item_count, feature_dim = arrived.shape
        tokens = arrived.reshape(num_slots * item_count, feature_dim)
        gate_val = jnp.dot(tokens, gate_mat, preferred_element_type=jnp.float32)
        up_val = jnp.dot(tokens, up_mat, preferred_element_type=jnp.float32)
        activated = (jax.nn.silu(gate_val) * up_val).astype(jnp.bfloat16)
        expert_out = (
            jnp.einsum("sf,gfc->sgc", activated, down_blocks, preferred_element_type=jnp.float32)
            .astype(jnp.bfloat16)
            .reshape(activated.shape[0], -1)
        )
        returned = lax.all_to_all(
            expert_out.reshape(num_slots, item_count, feature_dim),
            "expert",
            split_axis=0,
            concat_axis=0,
            tiled=True,
        )
        combined = jnp.dot(
            mixing,
            returned.reshape(experts_all * capacity, -1).astype(jnp.float32),
            precision=lax.Precision.HIGHEST,
        )
        results.append((hidden.astype(jnp.float32) + combined).astype(jnp.bfloat16))
    return jnp.stack(results)


def solution(mesh):
    in_specs = (
        P(None, ("group", "expert"), None),
        P(None, ("group", "expert"), None),
        P(None, ("group", "expert"), None),
        P(None, ("group", "expert"), None),
        P(("group", "expert"), None, None),
        P(("group", "expert"), None, None),
        P(("group", "expert")),
        P(None, ("group", "expert"), None),
        P(None, ("group", "expert"), None),
        P("expert", "group", None),
        P("expert", "group", None),
        P("expert", None, "group"),
    )
    out_specs = P(None, ("group", "expert"), None)
    return jax.shard_map(shards, mesh=mesh, in_specs=in_specs, out_specs=out_specs, check_vma=False)
```

```python
import jax
import jax.numpy as jnp
from jax import lax
from jax.sharding import PartitionSpec as P

HEADS = 32
KV_HEADS = 2
HEAD_DIM = 64
TOPK = 8
CACHE = 384
STEPS = 3


def attend_rows(query_vals, key_rows, value_rows, cache_ok, fresh_keys, fresh_values):
    factor = HEAD_DIM ** (-0.5)
    old_scores = (
        jnp.einsum("bkgd,bjkd->bkgj", query_vals, key_rows, preferred_element_type=jnp.float32)
        * factor
    )
    old_scores = jnp.where(cache_ok[:, None, None, :], old_scores, -1e30)
    new_scores = (
        jnp.einsum("bkgd,bjkd->bkgj", query_vals, fresh_keys, preferred_element_type=jnp.float32)
        * factor
    )
    highest = jnp.maximum(
        jnp.max(old_scores, axis=-1, keepdims=True), jnp.max(new_scores, axis=-1, keepdims=True)
    )
    old_weights = jnp.exp(old_scores - highest)
    new_weights = jnp.exp(new_scores - highest)
    denom_sum = jnp.sum(old_weights, axis=-1, keepdims=True) + jnp.sum(
        new_weights, axis=-1, keepdims=True
    )
    old_probs = (old_weights / denom_sum).astype(jnp.bfloat16)
    new_probs = (new_weights / denom_sum).astype(jnp.bfloat16)
    attended = jnp.einsum(
        "bkgj,bjkd->bkgd", old_probs, value_rows, preferred_element_type=jnp.float32
    )
    return attended + jnp.einsum(
        "bkgj,bjkd->bkgd", new_probs, fresh_values, preferred_element_type=jnp.float32
    )


def shards(
    inputs,
    queries,
    new_keys,
    new_values,
    key_cache,
    value_cache,
    cache_lengths,
    expert_ids,
    route_weights,
    w_gate,
    w_up,
    w_down,
):
    experts_all = lax.axis_size("expert")
    rows_dev = inputs.shape[1]
    per_group = HEADS // KV_HEADS
    capacity = max(2, 2 * rows_dev * TOPK // experts_all)
    shares = lax.axis_size("group")

    def gather_shares(weight):
        copies = jnp.broadcast_to(weight, (shares,) + weight.shape[1:])
        return lax.all_to_all(copies, "group", split_axis=0, concat_axis=0, tiled=True)

    gate_mat = gather_shares(w_gate).reshape(-1, w_gate.shape[2])
    up_mat = gather_shares(w_up).reshape(-1, w_up.shape[2])
    down_blocks = gather_shares(w_down)
    key_rows = key_cache.reshape(rows_dev, CACHE, KV_HEADS, HEAD_DIM)
    value_rows = value_cache.reshape(rows_dev, CACHE, KV_HEADS, HEAD_DIM)
    cache_ok = jnp.arange(CACHE, dtype=jnp.int32)[None, :] < cache_lengths[:, None]
    slot_columns = jnp.arange(experts_all * capacity, dtype=jnp.int32)
    expert_range = jnp.arange(experts_all, dtype=jnp.int32)
    outgoing_steps = []
    mixing_steps = []
    hidden_steps = []
    for step_index in range(STEPS):
        fresh = step_index + 1
        fresh_keys = jnp.swapaxes(new_keys[:fresh], 0, 1).reshape(
            rows_dev, fresh, KV_HEADS, HEAD_DIM
        )
        fresh_values = jnp.swapaxes(new_values[:fresh], 0, 1).reshape(
            rows_dev, fresh, KV_HEADS, HEAD_DIM
        )
        query_vals = queries[step_index].reshape(rows_dev, KV_HEADS, per_group, HEAD_DIM)
        attended = attend_rows(query_vals, key_rows, value_rows, cache_ok, fresh_keys, fresh_values)
        hidden = (inputs[step_index].astype(jnp.float32) + attended.reshape(rows_dev, -1)).astype(
            jnp.bfloat16
        )
        chosen = expert_ids[step_index].reshape(-1)
        onehot = (chosen[:, None] == expert_range[None, :]).astype(jnp.int32)
        before = jnp.cumsum(onehot, axis=0) - onehot
        slot_rank = jnp.sum(before * onehot, axis=1)
        target = chosen * capacity + slot_rank
        placed = (target[:, None] == slot_columns[None, :]).reshape(rows_dev, TOPK, -1)
        spread = jnp.any(placed, axis=1).astype(jnp.bfloat16)
        outgoing = jnp.einsum(
            "rc,rd->cd", spread, hidden, preferred_element_type=jnp.float32
        ).astype(jnp.bfloat16)
        outgoing_steps.append(outgoing.reshape(experts_all, capacity, -1))
        mixing_steps.append(
            jnp.sum(jnp.where(placed, route_weights[step_index][:, :, None], 0.0), axis=1)
        )
        hidden_steps.append(hidden)
    outgoing_all = jnp.stack(outgoing_steps, axis=1).reshape(experts_all, STEPS * capacity, -1)
    arrived = lax.all_to_all(outgoing_all, "expert", split_axis=0, concat_axis=0, tiled=True)
    num_slots, item_count, feature_dim = arrived.shape
    tokens = arrived.reshape(num_slots * item_count, feature_dim)
    gate_val = jnp.dot(tokens, gate_mat, preferred_element_type=jnp.float32)
    up_val = jnp.dot(tokens, up_mat, preferred_element_type=jnp.float32)
    activated = (jax.nn.silu(gate_val) * up_val).astype(jnp.bfloat16)
    expert_out = jnp.einsum(
        "sf,gfc->sgc", activated, down_blocks, preferred_element_type=jnp.float32
    ).astype(jnp.bfloat16)
    returned = lax.all_to_all(
        expert_out.reshape(num_slots, item_count, feature_dim),
        "expert",
        split_axis=0,
        concat_axis=0,
        tiled=True,
    ).reshape(experts_all, STEPS, capacity, feature_dim)
    results = []
    for step_index in range(STEPS):
        combined = jnp.dot(
            mixing_steps[step_index],
            returned[:, step_index].reshape(experts_all * capacity, -1).astype(jnp.float32),
            precision=lax.Precision.HIGHEST,
        )
        results.append((hidden_steps[step_index].astype(jnp.float32) + combined).astype(jnp.bfloat16))
    return jnp.stack(results)


def solution(mesh):
    in_specs = (
        P(None, ("group", "expert"), None),
        P(None, ("group", "expert"), None),
        P(None, ("group", "expert"), None),
        P(None, ("group", "expert"), None),
        P(("group", "expert"), None, None),
        P(("group", "expert"), None, None),
        P(("group", "expert")),
        P(None, ("group", "expert"), None),
        P(None, ("group", "expert"), None),
        P("expert", "group", None),
        P("expert", "group", None),
        P("expert", None, "group"),
    )
    out_specs = P(None, ("group", "expert"), None)
    return jax.shard_map(shards, mesh=mesh, in_specs=in_specs, out_specs=out_specs, check_vma=False)
```

```python
import jax
import jax.numpy as jnp
from jax import lax
from jax.sharding import PartitionSpec as P

HEADS = 32
KV_HEADS = 2
HEAD_DIM = 64
TOPK = 8
CACHE = 384
STEPS = 3


def attend_rows(query_vals, key_rows, value_rows, cache_ok, fresh_keys, fresh_values):
    factor = HEAD_DIM ** (-0.5)
    old_scores = (
        jnp.einsum("bkgd,bjkd->bkgj", query_vals, key_rows, preferred_element_type=jnp.float32)
        * factor
    )
    old_scores = jnp.where(cache_ok[:, None, None, :], old_scores, -1e30)
    new_scores = (
        jnp.einsum("bkgd,bjkd->bkgj", query_vals, fresh_keys, preferred_element_type=jnp.float32)
        * factor
    )
    highest = jnp.maximum(
        jnp.max(old_scores, axis=-1, keepdims=True), jnp.max(new_scores, axis=-1, keepdims=True)
    )
    old_weights = jnp.exp(old_scores - highest)
    new_weights = jnp.exp(new_scores - highest)
    denom_sum = jnp.sum(old_weights, axis=-1, keepdims=True) + jnp.sum(
        new_weights, axis=-1, keepdims=True
    )
    old_probs = (old_weights / denom_sum).astype(jnp.bfloat16)
    new_probs = (new_weights / denom_sum).astype(jnp.bfloat16)
    attended = jnp.einsum(
        "bkgj,bjkd->bkgd", old_probs, value_rows, preferred_element_type=jnp.float32
    )
    return attended + jnp.einsum(
        "bkgj,bjkd->bkgd", new_probs, fresh_values, preferred_element_type=jnp.float32
    )


def shards(
    inputs,
    queries,
    new_keys,
    new_values,
    key_cache,
    value_cache,
    cache_lengths,
    expert_ids,
    route_weights,
    w_gate,
    w_up,
    w_down,
):
    experts_all = lax.axis_size("expert")
    rows_dev = inputs.shape[1]
    per_group = HEADS // KV_HEADS
    capacity = max(2, 2 * rows_dev * TOPK // experts_all)
    shares = lax.axis_size("group")

    def gather_shares(weight):
        copies = jnp.broadcast_to(weight, (shares,) + weight.shape[1:])
        return lax.all_to_all(copies, "group", split_axis=0, concat_axis=0, tiled=True)

    gate_mat = gather_shares(w_gate).reshape(-1, w_gate.shape[2])
    up_mat = gather_shares(w_up).reshape(-1, w_up.shape[2])
    down_mat = lax.all_gather(w_down, "group", axis=2, tiled=True)[0]
    key_rows = key_cache.reshape(rows_dev, CACHE, KV_HEADS, HEAD_DIM)
    value_rows = value_cache.reshape(rows_dev, CACHE, KV_HEADS, HEAD_DIM)
    cache_ok = jnp.arange(CACHE, dtype=jnp.int32)[None, :] < cache_lengths[:, None]
    slot_columns = jnp.arange(experts_all * capacity, dtype=jnp.int32)
    expert_range = jnp.arange(experts_all, dtype=jnp.int32)
    results = []
    for step_index in range(STEPS):
        fresh = step_index + 1
        fresh_keys = jnp.swapaxes(new_keys[:fresh], 0, 1).reshape(
            rows_dev, fresh, KV_HEADS, HEAD_DIM
        )
        fresh_values = jnp.swapaxes(new_values[:fresh], 0, 1).reshape(
            rows_dev, fresh, KV_HEADS, HEAD_DIM
        )
        query_vals = queries[step_index].reshape(rows_dev, KV_HEADS, per_group, HEAD_DIM)
        attended = attend_rows(query_vals, key_rows, value_rows, cache_ok, fresh_keys, fresh_values)
        hidden = (inputs[step_index].astype(jnp.float32) + attended.reshape(rows_dev, -1)).astype(
            jnp.bfloat16
        )
        chosen = expert_ids[step_index].reshape(-1)
        onehot = (chosen[:, None] == expert_range[None, :]).astype(jnp.int32)
        before = jnp.cumsum(onehot, axis=0) - onehot
        slot_rank = jnp.sum(before * onehot, axis=1)
        target = chosen * capacity + slot_rank
        placed = (target[:, None] == slot_columns[None, :]).reshape(rows_dev, TOPK, -1)
        spread = jnp.any(placed, axis=1).astype(jnp.bfloat16)
        outgoing = jnp.einsum(
            "rc,rd->cd", spread, hidden, preferred_element_type=jnp.float32
        ).astype(jnp.bfloat16)
        outgoing = outgoing.reshape(experts_all, capacity, -1)
        mixing = jnp.sum(jnp.where(placed, route_weights[step_index][:, :, None], 0.0), axis=1)
        arrived = lax.all_to_all(outgoing, "expert", split_axis=0, concat_axis=0, tiled=True)
        num_slots, item_count, feature_dim = arrived.shape
        tokens = arrived.reshape(num_slots * item_count, feature_dim)
        gate_val = jnp.dot(tokens, gate_mat, preferred_element_type=jnp.float32)
        up_val = jnp.dot(tokens, up_mat, preferred_element_type=jnp.float32)
        activated = (jax.nn.silu(gate_val) * up_val).astype(jnp.bfloat16)
        expert_out = jnp.dot(activated, down_mat, preferred_element_type=jnp.float32).astype(
            jnp.bfloat16
        )
        returned = lax.all_to_all(
            expert_out.reshape(num_slots, item_count, feature_dim),
            "expert",
            split_axis=0,
            concat_axis=0,
            tiled=True,
        )
        combined = jnp.dot(
            mixing,
            returned.reshape(experts_all * capacity, -1).astype(jnp.float32),
            precision=lax.Precision.HIGHEST,
        )
        results.append((hidden.astype(jnp.float32) + combined).astype(jnp.bfloat16))
    return jnp.stack(results)


def solution(mesh):
    in_specs = (
        P(None, ("group", "expert"), None),
        P(None, ("group", "expert"), None),
        P(None, ("group", "expert"), None),
        P(None, ("group", "expert"), None),
        P(("group", "expert"), None, None),
        P(("group", "expert"), None, None),
        P(("group", "expert")),
        P(None, ("group", "expert"), None),
        P(None, ("group", "expert"), None),
        P("expert", "group", None),
        P("expert", "group", None),
        P("expert", None, "group"),
    )
    out_specs = P(None, ("group", "expert"), None)
    return jax.shard_map(shards, mesh=mesh, in_specs=in_specs, out_specs=out_specs, check_vma=False)
```

```python
import jax
import jax.numpy as jnp
from jax import lax
from jax.sharding import PartitionSpec as P

HEADS = 32
KV_HEADS = 2
HEAD_DIM = 64
TOPK = 8
CACHE = 384
STEPS = 3


def attend_rows(query_vals, key_rows, value_rows, cache_ok, fresh_keys, fresh_values):
    factor = HEAD_DIM ** (-0.5)
    old_scores = (
        jnp.einsum("bkgd,bjkd->bkgj", query_vals, key_rows, preferred_element_type=jnp.float32)
        * factor
    )
    old_scores = jnp.where(cache_ok[:, None, None, :], old_scores, -1e30)
    new_scores = (
        jnp.einsum("bkgd,bjkd->bkgj", query_vals, fresh_keys, preferred_element_type=jnp.float32)
        * factor
    )
    highest = jnp.maximum(
        jnp.max(old_scores, axis=-1, keepdims=True), jnp.max(new_scores, axis=-1, keepdims=True)
    )
    old_weights = jnp.exp(old_scores - highest)
    new_weights = jnp.exp(new_scores - highest)
    denom_sum = jnp.sum(old_weights, axis=-1, keepdims=True) + jnp.sum(
        new_weights, axis=-1, keepdims=True
    )
    old_probs = (old_weights / denom_sum).astype(jnp.bfloat16)
    new_probs = (new_weights / denom_sum).astype(jnp.bfloat16)
    attended = jnp.einsum(
        "bkgj,bjkd->bkgd", old_probs, value_rows, preferred_element_type=jnp.float32
    )
    return attended + jnp.einsum(
        "bkgj,bjkd->bkgd", new_probs, fresh_values, preferred_element_type=jnp.float32
    )


def shards(
    inputs,
    queries,
    new_keys,
    new_values,
    key_cache,
    value_cache,
    cache_lengths,
    expert_ids,
    route_weights,
    w_gate,
    w_up,
    w_down,
):
    experts_all = lax.axis_size("expert")
    rows_dev = inputs.shape[1]
    per_group = HEADS // KV_HEADS
    capacity = max(2, 2 * rows_dev * TOPK // experts_all)
    shares = lax.axis_size("group")

    here = lax.axis_index("group")

    def gather_shares(weight):
        received = [weight[0]]
        for shift in range(1, shares):
            pairs = [(i, (i + shift) % shares) for i in range(shares)]
            received.append(lax.ppermute(weight[0], "group", pairs))
        return jnp.roll(jnp.stack(received[::-1]), here + 1, axis=0)

    gate_mat = gather_shares(w_gate).reshape(-1, w_gate.shape[2])
    up_mat = gather_shares(w_up).reshape(-1, w_up.shape[2])
    down_blocks = gather_shares(w_down)
    key_rows = key_cache.reshape(rows_dev, CACHE, KV_HEADS, HEAD_DIM)
    value_rows = value_cache.reshape(rows_dev, CACHE, KV_HEADS, HEAD_DIM)
    cache_ok = jnp.arange(CACHE, dtype=jnp.int32)[None, :] < cache_lengths[:, None]
    slot_columns = jnp.arange(experts_all * capacity, dtype=jnp.int32)
    expert_range = jnp.arange(experts_all, dtype=jnp.int32)
    results = []
    for step_index in range(STEPS):
        fresh = step_index + 1
        fresh_keys = jnp.swapaxes(new_keys[:fresh], 0, 1).reshape(
            rows_dev, fresh, KV_HEADS, HEAD_DIM
        )
        fresh_values = jnp.swapaxes(new_values[:fresh], 0, 1).reshape(
            rows_dev, fresh, KV_HEADS, HEAD_DIM
        )
        query_vals = queries[step_index].reshape(rows_dev, KV_HEADS, per_group, HEAD_DIM)
        attended = attend_rows(query_vals, key_rows, value_rows, cache_ok, fresh_keys, fresh_values)
        hidden = (inputs[step_index].astype(jnp.float32) + attended.reshape(rows_dev, -1)).astype(
            jnp.bfloat16
        )
        chosen = expert_ids[step_index].reshape(-1)
        onehot = (chosen[:, None] == expert_range[None, :]).astype(jnp.int32)
        before = jnp.cumsum(onehot, axis=0) - onehot
        slot_rank = jnp.sum(before * onehot, axis=1)
        target = chosen * capacity + slot_rank
        placed = (target[:, None] == slot_columns[None, :]).reshape(rows_dev, TOPK, -1)
        spread = jnp.any(placed, axis=1).astype(jnp.bfloat16)
        outgoing = jnp.einsum(
            "rc,rd->cd", spread, hidden, preferred_element_type=jnp.float32
        ).astype(jnp.bfloat16)
        outgoing = outgoing.reshape(experts_all, capacity, -1)
        mixing = jnp.sum(jnp.where(placed, route_weights[step_index][:, :, None], 0.0), axis=1)
        arrived = lax.all_to_all(outgoing, "expert", split_axis=0, concat_axis=0, tiled=True)
        num_slots, item_count, feature_dim = arrived.shape
        tokens = arrived.reshape(num_slots * item_count, feature_dim)
        gate_val = jnp.dot(tokens, gate_mat, preferred_element_type=jnp.float32)
        up_val = jnp.dot(tokens, up_mat, preferred_element_type=jnp.float32)
        activated = (jax.nn.silu(gate_val) * up_val).astype(jnp.bfloat16)
        expert_out = (
            jnp.einsum("sf,gfc->sgc", activated, down_blocks, preferred_element_type=jnp.float32)
            .astype(jnp.bfloat16)
            .reshape(activated.shape[0], -1)
        )
        returned = lax.all_to_all(
            expert_out.reshape(num_slots, item_count, feature_dim),
            "expert",
            split_axis=0,
            concat_axis=0,
            tiled=True,
        )
        combined = jnp.dot(
            mixing,
            returned.reshape(experts_all * capacity, -1).astype(jnp.float32),
            precision=lax.Precision.HIGHEST,
        )
        results.append((hidden.astype(jnp.float32) + combined).astype(jnp.bfloat16))
    return jnp.stack(results)


def solution(mesh):
    in_specs = (
        P(None, ("group", "expert"), None),
        P(None, ("group", "expert"), None),
        P(None, ("group", "expert"), None),
        P(None, ("group", "expert"), None),
        P(("group", "expert"), None, None),
        P(("group", "expert"), None, None),
        P(("group", "expert")),
        P(None, ("group", "expert"), None),
        P(None, ("group", "expert"), None),
        P("expert", "group", None),
        P("expert", "group", None),
        P("expert", None, "group"),
    )
    out_specs = P(None, ("group", "expert"), None)
    return jax.shard_map(shards, mesh=mesh, in_specs=in_specs, out_specs=out_specs, check_vma=False)
```

```python
import jax
import jax.numpy as jnp
from jax import lax
from jax.sharding import PartitionSpec as P

HEADS = 32
KV_HEADS = 2
HEAD_DIM = 64
TOPK = 8
CACHE = 384
STEPS = 3


def attend_rows(query_vals, key_rows, value_rows, cache_ok, fresh_keys, fresh_values):
    factor = HEAD_DIM ** (-0.5)
    old_scores = (
        jnp.einsum("bkgd,bjkd->bkgj", query_vals, key_rows, preferred_element_type=jnp.float32)
        * factor
    )
    old_scores = jnp.where(cache_ok[:, None, None, :], old_scores, -1e30)
    new_scores = (
        jnp.einsum("bkgd,bjkd->bkgj", query_vals, fresh_keys, preferred_element_type=jnp.float32)
        * factor
    )
    highest = jnp.maximum(
        jnp.max(old_scores, axis=-1, keepdims=True), jnp.max(new_scores, axis=-1, keepdims=True)
    )
    old_weights = jnp.exp(old_scores - highest)
    new_weights = jnp.exp(new_scores - highest)
    denom_sum = jnp.sum(old_weights, axis=-1, keepdims=True) + jnp.sum(
        new_weights, axis=-1, keepdims=True
    )
    old_probs = (old_weights / denom_sum).astype(jnp.bfloat16)
    new_probs = (new_weights / denom_sum).astype(jnp.bfloat16)
    attended = jnp.einsum(
        "bkgj,bjkd->bkgd", old_probs, value_rows, preferred_element_type=jnp.float32
    )
    return attended + jnp.einsum(
        "bkgj,bjkd->bkgd", new_probs, fresh_values, preferred_element_type=jnp.float32
    )


def shards(
    inputs,
    queries,
    new_keys,
    new_values,
    key_cache,
    value_cache,
    cache_lengths,
    expert_ids,
    route_weights,
    w_gate,
    w_up,
    w_down,
):
    experts_all = lax.axis_size("expert")
    rows_dev = inputs.shape[1]
    per_group = HEADS // KV_HEADS
    capacity = max(2, 2 * rows_dev * TOPK // experts_all)
    shares = lax.axis_size("group")

    here = lax.axis_index("group")

    local = jnp.stack([w_gate[0].reshape(-1), w_up[0].reshape(-1), w_down[0].reshape(-1)])
    received = [local]
    for shift in range(1, shares):
        pairs = [(i, (i + shift) % shares) for i in range(shares)]
        received.append(lax.ppermute(local, "group", pairs))
    gathered = jnp.roll(jnp.stack(received[::-1], axis=1), here + 1, axis=1)
    gate_mat = gathered[0].reshape(-1, w_gate.shape[2])
    up_mat = gathered[1].reshape(-1, w_up.shape[2])
    down_blocks = gathered[2].reshape(shares, w_down.shape[1], w_down.shape[2])
    key_rows = key_cache.reshape(rows_dev, CACHE, KV_HEADS, HEAD_DIM)
    value_rows = value_cache.reshape(rows_dev, CACHE, KV_HEADS, HEAD_DIM)
    cache_ok = jnp.arange(CACHE, dtype=jnp.int32)[None, :] < cache_lengths[:, None]
    slot_columns = jnp.arange(experts_all * capacity, dtype=jnp.int32)
    expert_range = jnp.arange(experts_all, dtype=jnp.int32)
    results = []
    for step_index in range(STEPS):
        fresh = step_index + 1
        fresh_keys = jnp.swapaxes(new_keys[:fresh], 0, 1).reshape(
            rows_dev, fresh, KV_HEADS, HEAD_DIM
        )
        fresh_values = jnp.swapaxes(new_values[:fresh], 0, 1).reshape(
            rows_dev, fresh, KV_HEADS, HEAD_DIM
        )
        query_vals = queries[step_index].reshape(rows_dev, KV_HEADS, per_group, HEAD_DIM)
        attended = attend_rows(query_vals, key_rows, value_rows, cache_ok, fresh_keys, fresh_values)
        hidden = (inputs[step_index].astype(jnp.float32) + attended.reshape(rows_dev, -1)).astype(
            jnp.bfloat16
        )
        chosen = expert_ids[step_index].reshape(-1)
        onehot = (chosen[:, None] == expert_range[None, :]).astype(jnp.int32)
        before = jnp.cumsum(onehot, axis=0) - onehot
        slot_rank = jnp.sum(before * onehot, axis=1)
        target = chosen * capacity + slot_rank
        placed = (target[:, None] == slot_columns[None, :]).reshape(rows_dev, TOPK, -1)
        spread = jnp.any(placed, axis=1).astype(jnp.bfloat16)
        outgoing = jnp.einsum(
            "rc,rd->cd", spread, hidden, preferred_element_type=jnp.float32
        ).astype(jnp.bfloat16)
        outgoing = outgoing.reshape(experts_all, capacity, -1)
        mixing = jnp.sum(jnp.where(placed, route_weights[step_index][:, :, None], 0.0), axis=1)
        arrived = lax.all_to_all(outgoing, "expert", split_axis=0, concat_axis=0, tiled=True)
        num_slots, item_count, feature_dim = arrived.shape
        tokens = arrived.reshape(num_slots * item_count, feature_dim)
        gate_val = jnp.dot(tokens, gate_mat, preferred_element_type=jnp.float32)
        up_val = jnp.dot(tokens, up_mat, preferred_element_type=jnp.float32)
        activated = (jax.nn.silu(gate_val) * up_val).astype(jnp.bfloat16)
        expert_out = (
            jnp.einsum("sf,gfc->sgc", activated, down_blocks, preferred_element_type=jnp.float32)
            .astype(jnp.bfloat16)
            .reshape(activated.shape[0], -1)
        )
        returned = lax.all_to_all(
            expert_out.reshape(num_slots, item_count, feature_dim),
            "expert",
            split_axis=0,
            concat_axis=0,
            tiled=True,
        )
        combined = jnp.dot(
            mixing,
            returned.reshape(experts_all * capacity, -1).astype(jnp.float32),
            precision=lax.Precision.HIGHEST,
        )
        results.append((hidden.astype(jnp.float32) + combined).astype(jnp.bfloat16))
    return jnp.stack(results)


def solution(mesh):
    in_specs = (
        P(None, ("group", "expert"), None),
        P(None, ("group", "expert"), None),
        P(None, ("group", "expert"), None),
        P(None, ("group", "expert"), None),
        P(("group", "expert"), None, None),
        P(("group", "expert"), None, None),
        P(("group", "expert")),
        P(None, ("group", "expert"), None),
        P(None, ("group", "expert"), None),
        P("expert", "group", None),
        P("expert", "group", None),
        P("expert", None, "group"),
    )
    out_specs = P(None, ("group", "expert"), None)
    return jax.shard_map(shards, mesh=mesh, in_specs=in_specs, out_specs=out_specs, check_vma=False)
```

```python
import jax
import jax.numpy as jnp
from jax import lax
from jax.experimental import pallas as pl
from jax.experimental.pallas import tpu as pltpu
from jax.sharding import PartitionSpec as P

HEADS = 32
KV_HEADS = 2
HEAD_DIM = 64
TOPK = 8
CACHE = 384
STEPS = 3


def attend_rows(query_vals, key_rows, value_rows, cache_ok, fresh_keys, fresh_values):
    factor = HEAD_DIM ** (-0.5)
    old_scores = (
        jnp.einsum("bkgd,bjkd->bkgj", query_vals, key_rows, preferred_element_type=jnp.float32)
        * factor
    )
    old_scores = jnp.where(cache_ok[:, None, None, :], old_scores, -1e30)
    new_scores = (
        jnp.einsum("bkgd,bjkd->bkgj", query_vals, fresh_keys, preferred_element_type=jnp.float32)
        * factor
    )
    highest = jnp.maximum(
        jnp.max(old_scores, axis=-1, keepdims=True), jnp.max(new_scores, axis=-1, keepdims=True)
    )
    old_weights = jnp.exp(old_scores - highest)
    new_weights = jnp.exp(new_scores - highest)
    denom_sum = jnp.sum(old_weights, axis=-1, keepdims=True) + jnp.sum(
        new_weights, axis=-1, keepdims=True
    )
    old_probs = (old_weights / denom_sum).astype(jnp.bfloat16)
    new_probs = (new_weights / denom_sum).astype(jnp.bfloat16)
    attended = jnp.einsum(
        "bkgj,bjkd->bkgd", old_probs, value_rows, preferred_element_type=jnp.float32
    )
    return attended + jnp.einsum(
        "bkgj,bjkd->bkgd", new_probs, fresh_values, preferred_element_type=jnp.float32
    )


def expert_ffn(here, tokens, gate_parts, up_parts, down_parts):
    shares = len(gate_parts)
    slots, width = tokens.shape
    block = width // shares
    token_blocks = tokens.reshape(slots, shares, block).transpose(1, 0, 2)

    def kernel(here_ref, tok_ref, *refs):
        gates, ups, downs = refs[:shares], refs[shares:2 * shares], refs[2 * shares:3 * shares]
        out_ref = refs[3 * shares]
        origin = here_ref[0]
        gate = up = None
        for k in range(shares):
            piece = tok_ref[(origin - k + shares) % shares]
            g = jnp.dot(piece, gates[k][...], preferred_element_type=jnp.float32)
            u = jnp.dot(piece, ups[k][...], preferred_element_type=jnp.float32)
            gate = g if gate is None else gate + g
            up = u if up is None else up + u
        activated = (gate / (1.0 + jnp.exp(-gate)) * up).astype(jnp.bfloat16)
        for k in range(shares):
            out_ref[(origin - k + shares) % shares] = jnp.dot(
                activated, downs[k][...], preferred_element_type=jnp.float32
            ).astype(out_ref.dtype)

    vmem = pl.BlockSpec(memory_space=pltpu.VMEM)
    out = pl.pallas_call(
        kernel,
        out_shape=jax.ShapeDtypeStruct((shares, slots, block), jnp.bfloat16),
        in_specs=[pl.BlockSpec(memory_space=pltpu.SMEM)] + [vmem] * (1 + 3 * shares),
        out_specs=vmem,
    )(jnp.reshape(here, (1,)).astype(jnp.int32), token_blocks, *gate_parts, *up_parts, *down_parts)
    return out.transpose(1, 0, 2).reshape(slots, width)


def shards(
    inputs,
    queries,
    new_keys,
    new_values,
    key_cache,
    value_cache,
    cache_lengths,
    expert_ids,
    route_weights,
    w_gate,
    w_up,
    w_down,
):
    experts_all = lax.axis_size("expert")
    rows_dev = inputs.shape[1]
    per_group = HEADS // KV_HEADS
    capacity = max(2, 2 * rows_dev * TOPK // experts_all)
    shares = lax.axis_size("group")

    here = lax.axis_index("group")

    def gather_shares(weight):
        received = [weight[0]]
        for shift in range(1, shares):
            pairs = [(i, (i + shift) % shares) for i in range(shares)]
            received.append(lax.ppermute(weight[0], "group", pairs))
        return received

    gate_parts = gather_shares(w_gate)
    up_parts = gather_shares(w_up)
    down_parts = gather_shares(w_down)
    key_rows = key_cache.reshape(rows_dev, CACHE, KV_HEADS, HEAD_DIM)
    value_rows = value_cache.reshape(rows_dev, CACHE, KV_HEADS, HEAD_DIM)
    cache_ok = jnp.arange(CACHE, dtype=jnp.int32)[None, :] < cache_lengths[:, None]
    slot_columns = jnp.arange(experts_all * capacity, dtype=jnp.int32)
    expert_range = jnp.arange(experts_all, dtype=jnp.int32)
    results = []
    for step_index in range(STEPS):
        fresh = step_index + 1
        fresh_keys = jnp.swapaxes(new_keys[:fresh], 0, 1).reshape(
            rows_dev, fresh, KV_HEADS, HEAD_DIM
        )
        fresh_values = jnp.swapaxes(new_values[:fresh], 0, 1).reshape(
            rows_dev, fresh, KV_HEADS, HEAD_DIM
        )
        query_vals = queries[step_index].reshape(rows_dev, KV_HEADS, per_group, HEAD_DIM)
        attended = attend_rows(query_vals, key_rows, value_rows, cache_ok, fresh_keys, fresh_values)
        hidden = (inputs[step_index].astype(jnp.float32) + attended.reshape(rows_dev, -1)).astype(
            jnp.bfloat16
        )
        chosen = expert_ids[step_index].reshape(-1)
        onehot = (chosen[:, None] == expert_range[None, :]).astype(jnp.int32)
        before = jnp.cumsum(onehot, axis=0) - onehot
        slot_rank = jnp.sum(before * onehot, axis=1)
        target = chosen * capacity + slot_rank
        placed = (target[:, None] == slot_columns[None, :]).reshape(rows_dev, TOPK, -1)
        spread = jnp.any(placed, axis=1).astype(jnp.bfloat16)
        outgoing = jnp.einsum(
            "rc,rd->cd", spread, hidden, preferred_element_type=jnp.float32
        ).astype(jnp.bfloat16)
        outgoing = outgoing.reshape(experts_all, capacity, -1)
        mixing = jnp.sum(jnp.where(placed, route_weights[step_index][:, :, None], 0.0), axis=1)
        arrived = lax.all_to_all(outgoing, "expert", split_axis=0, concat_axis=0, tiled=True)
        num_slots, item_count, feature_dim = arrived.shape
        tokens = arrived.reshape(num_slots * item_count, feature_dim)
        expert_out = expert_ffn(here, tokens, gate_parts, up_parts, down_parts)
        returned = lax.all_to_all(
            expert_out.reshape(num_slots, item_count, feature_dim),
            "expert",
            split_axis=0,
            concat_axis=0,
            tiled=True,
        )
        combined = jnp.dot(
            mixing,
            returned.reshape(experts_all * capacity, -1).astype(jnp.float32),
            precision=lax.Precision.HIGHEST,
        )
        results.append((hidden.astype(jnp.float32) + combined).astype(jnp.bfloat16))
    return jnp.stack(results)


def solution(mesh):
    in_specs = (
        P(None, ("group", "expert"), None),
        P(None, ("group", "expert"), None),
        P(None, ("group", "expert"), None),
        P(None, ("group", "expert"), None),
        P(("group", "expert"), None, None),
        P(("group", "expert"), None, None),
        P(("group", "expert")),
        P(None, ("group", "expert"), None),
        P(None, ("group", "expert"), None),
        P("expert", "group", None),
        P("expert", "group", None),
        P("expert", None, "group"),
    )
    out_specs = P(None, ("group", "expert"), None)
    return jax.shard_map(shards, mesh=mesh, in_specs=in_specs, out_specs=out_specs, check_vma=False)
```

```python
import jax
import jax.numpy as jnp
from jax import lax
from jax.experimental import pallas as pl
from jax.experimental.pallas import tpu as pltpu
from jax.sharding import PartitionSpec as P

HEADS = 32
KV_HEADS = 2
HEAD_DIM = 64
TOPK = 8
CACHE = 384
STEPS = 3


def attend_rows(query_vals, key_rows, value_rows, cache_ok, fresh_keys, fresh_values):
    factor = HEAD_DIM ** (-0.5)
    old_scores = (
        jnp.einsum("bkgd,bjkd->bkgj", query_vals, key_rows, preferred_element_type=jnp.float32)
        * factor
    )
    old_scores = jnp.where(cache_ok[:, None, None, :], old_scores, -1e30)
    new_scores = (
        jnp.einsum("bkgd,bjkd->bkgj", query_vals, fresh_keys, preferred_element_type=jnp.float32)
        * factor
    )
    highest = jnp.maximum(
        jnp.max(old_scores, axis=-1, keepdims=True), jnp.max(new_scores, axis=-1, keepdims=True)
    )
    old_weights = jnp.exp(old_scores - highest)
    new_weights = jnp.exp(new_scores - highest)
    denom_sum = jnp.sum(old_weights, axis=-1, keepdims=True) + jnp.sum(
        new_weights, axis=-1, keepdims=True
    )
    old_probs = (old_weights / denom_sum).astype(jnp.bfloat16)
    new_probs = (new_weights / denom_sum).astype(jnp.bfloat16)
    attended = jnp.einsum(
        "bkgj,bjkd->bkgd", old_probs, value_rows, preferred_element_type=jnp.float32
    )
    return attended + jnp.einsum(
        "bkgj,bjkd->bkgd", new_probs, fresh_values, preferred_element_type=jnp.float32
    )


def expert_ffn(here, tokens, gate_stack, up_stack, down_stack):
    shares, block, hidden_units = gate_stack.shape
    slots, width = tokens.shape
    token_blocks = tokens.reshape(slots, shares, block).transpose(1, 0, 2)

    def kernel(here_ref, tok_ref, gate_ref, up_ref, down_ref, out_ref):
        origin = here_ref[0]
        gate = up = None
        for k in range(shares):
            piece = tok_ref[(origin - k + shares) % shares]
            g = jnp.dot(piece, gate_ref[k], preferred_element_type=jnp.float32)
            u = jnp.dot(piece, up_ref[k], preferred_element_type=jnp.float32)
            gate = g if gate is None else gate + g
            up = u if up is None else up + u
        activated = (gate / (1.0 + jnp.exp(-gate)) * up).astype(jnp.bfloat16)
        for k in range(shares):
            out_ref[(origin - k + shares) % shares] = jnp.dot(
                activated, down_ref[k], preferred_element_type=jnp.float32
            ).astype(out_ref.dtype)

    vmem = pl.BlockSpec(memory_space=pltpu.VMEM)
    out = pl.pallas_call(
        kernel,
        out_shape=jax.ShapeDtypeStruct((shares, slots, block), jnp.bfloat16),
        in_specs=[pl.BlockSpec(memory_space=pltpu.SMEM)] + [vmem] * 4,
        out_specs=vmem,
        cost_estimate=pl.CostEstimate(
            flops=6 * slots * width * hidden_units,
            transcendentals=slots * hidden_units,
            bytes_accessed=2 * (3 * width * hidden_units + 2 * slots * width),
        ),
    )(jnp.reshape(here, (1,)).astype(jnp.int32), token_blocks, gate_stack, up_stack, down_stack)
    return out.transpose(1, 0, 2).reshape(slots, width)


def shards(
    inputs,
    queries,
    new_keys,
    new_values,
    key_cache,
    value_cache,
    cache_lengths,
    expert_ids,
    route_weights,
    w_gate,
    w_up,
    w_down,
):
    experts_all = lax.axis_size("expert")
    rows_dev = inputs.shape[1]
    per_group = HEADS // KV_HEADS
    capacity = max(2, 2 * rows_dev * TOPK // experts_all)
    shares = lax.axis_size("group")

    here = lax.axis_index("group")

    def gather_shares(weight):
        received = [weight[0]]
        for shift in range(1, shares):
            pairs = [(i, (i + shift) % shares) for i in range(shares)]
            received.append(lax.ppermute(weight[0], "group", pairs))
        return jnp.stack(received)

    gate_stack = gather_shares(w_gate)
    up_stack = gather_shares(w_up)
    down_stack = gather_shares(w_down)
    key_rows = key_cache.reshape(rows_dev, CACHE, KV_HEADS, HEAD_DIM)
    value_rows = value_cache.reshape(rows_dev, CACHE, KV_HEADS, HEAD_DIM)
    cache_ok = jnp.arange(CACHE, dtype=jnp.int32)[None, :] < cache_lengths[:, None]
    slot_columns = jnp.arange(experts_all * capacity, dtype=jnp.int32)
    expert_range = jnp.arange(experts_all, dtype=jnp.int32)
    results = []
    for step_index in range(STEPS):
        fresh = step_index + 1
        fresh_keys = jnp.swapaxes(new_keys[:fresh], 0, 1).reshape(
            rows_dev, fresh, KV_HEADS, HEAD_DIM
        )
        fresh_values = jnp.swapaxes(new_values[:fresh], 0, 1).reshape(
            rows_dev, fresh, KV_HEADS, HEAD_DIM
        )
        query_vals = queries[step_index].reshape(rows_dev, KV_HEADS, per_group, HEAD_DIM)
        attended = attend_rows(query_vals, key_rows, value_rows, cache_ok, fresh_keys, fresh_values)
        hidden = (inputs[step_index].astype(jnp.float32) + attended.reshape(rows_dev, -1)).astype(
            jnp.bfloat16
        )
        chosen = expert_ids[step_index].reshape(-1)
        onehot = (chosen[:, None] == expert_range[None, :]).astype(jnp.int32)
        before = jnp.cumsum(onehot, axis=0) - onehot
        slot_rank = jnp.sum(before * onehot, axis=1)
        target = chosen * capacity + slot_rank
        placed = (target[:, None] == slot_columns[None, :]).reshape(rows_dev, TOPK, -1)
        spread = jnp.any(placed, axis=1).astype(jnp.bfloat16)
        outgoing = jnp.einsum(
            "rc,rd->cd", spread, hidden, preferred_element_type=jnp.float32
        ).astype(jnp.bfloat16)
        outgoing = outgoing.reshape(experts_all, capacity, -1)
        mixing = jnp.sum(jnp.where(placed, route_weights[step_index][:, :, None], 0.0), axis=1)
        arrived = lax.all_to_all(outgoing, "expert", split_axis=0, concat_axis=0, tiled=True)
        num_slots, item_count, feature_dim = arrived.shape
        tokens = arrived.reshape(num_slots * item_count, feature_dim)
        expert_out = expert_ffn(here, tokens, gate_stack, up_stack, down_stack)
        returned = lax.all_to_all(
            expert_out.reshape(num_slots, item_count, feature_dim),
            "expert",
            split_axis=0,
            concat_axis=0,
            tiled=True,
        )
        combined = jnp.dot(
            mixing,
            returned.reshape(experts_all * capacity, -1).astype(jnp.float32),
            precision=lax.Precision.HIGHEST,
        )
        results.append((hidden.astype(jnp.float32) + combined).astype(jnp.bfloat16))
    return jnp.stack(results)


def solution(mesh):
    in_specs = (
        P(None, ("group", "expert"), None),
        P(None, ("group", "expert"), None),
        P(None, ("group", "expert"), None),
        P(None, ("group", "expert"), None),
        P(("group", "expert"), None, None),
        P(("group", "expert"), None, None),
        P(("group", "expert")),
        P(None, ("group", "expert"), None),
        P(None, ("group", "expert"), None),
        P("expert", "group", None),
        P("expert", "group", None),
        P("expert", None, "group"),
    )
    out_specs = P(None, ("group", "expert"), None)
    return jax.shard_map(shards, mesh=mesh, in_specs=in_specs, out_specs=out_specs, check_vma=False)
```

```python
import jax
import jax.numpy as jnp
from jax import lax
from jax.experimental import pallas as pl
from jax.experimental.pallas import tpu as pltpu
from jax.sharding import PartitionSpec as P

HEADS = 32
KV_HEADS = 2
HEAD_DIM = 64
TOPK = 8
CACHE = 384
STEPS = 3


def attend_rows(query_vals, key_rows, value_rows, cache_ok, fresh_keys, fresh_values):
    factor = HEAD_DIM ** (-0.5)
    old_scores = (
        jnp.einsum("bkgd,bjkd->bkgj", query_vals, key_rows, preferred_element_type=jnp.float32)
        * factor
    )
    old_scores = jnp.where(cache_ok[:, None, None, :], old_scores, -1e30)
    new_scores = (
        jnp.einsum("bkgd,bjkd->bkgj", query_vals, fresh_keys, preferred_element_type=jnp.float32)
        * factor
    )
    highest = jnp.maximum(
        jnp.max(old_scores, axis=-1, keepdims=True), jnp.max(new_scores, axis=-1, keepdims=True)
    )
    old_weights = jnp.exp(old_scores - highest)
    new_weights = jnp.exp(new_scores - highest)
    denom_sum = jnp.sum(old_weights, axis=-1, keepdims=True) + jnp.sum(
        new_weights, axis=-1, keepdims=True
    )
    old_probs = (old_weights / denom_sum).astype(jnp.bfloat16)
    new_probs = (new_weights / denom_sum).astype(jnp.bfloat16)
    attended = jnp.einsum(
        "bkgj,bjkd->bkgd", old_probs, value_rows, preferred_element_type=jnp.float32
    )
    return attended + jnp.einsum(
        "bkgj,bjkd->bkgd", new_probs, fresh_values, preferred_element_type=jnp.float32
    )


def expert_ffn(sources, tokens, gate_stack, up_stack, down_stack):
    shares, block, hidden_units = gate_stack.shape
    slots, width = tokens.shape
    token_blocks = tokens.reshape(slots, shares, block).transpose(1, 0, 2)

    def kernel(source_ref, tok_ref, gate_ref, up_ref, down_ref, out_ref):
        gate = up = None
        for k in range(shares):
            piece = tok_ref[source_ref[k]]
            g = jnp.dot(piece, gate_ref[k], preferred_element_type=jnp.float32)
            u = jnp.dot(piece, up_ref[k], preferred_element_type=jnp.float32)
            gate = g if gate is None else gate + g
            up = u if up is None else up + u
        activated = (gate / (1.0 + jnp.exp(-gate)) * up).astype(jnp.bfloat16)
        for k in range(shares):
            out_ref[source_ref[k]] = jnp.dot(
                activated, down_ref[k], preferred_element_type=jnp.float32
            ).astype(out_ref.dtype)

    vmem = pl.BlockSpec(memory_space=pltpu.VMEM)
    out = pl.pallas_call(
        kernel,
        out_shape=jax.ShapeDtypeStruct((shares, slots, block), jnp.bfloat16),
        in_specs=[pl.BlockSpec(memory_space=pltpu.SMEM)] + [vmem] * 4,
        out_specs=vmem,
        cost_estimate=pl.CostEstimate(
            flops=6 * slots * width * hidden_units,
            transcendentals=slots * hidden_units,
            bytes_accessed=2 * (3 * width * hidden_units + 2 * slots * width),
        ),
    )(sources, token_blocks, gate_stack, up_stack, down_stack)
    return out.transpose(1, 0, 2).reshape(slots, width)


def shards(
    inputs,
    queries,
    new_keys,
    new_values,
    key_cache,
    value_cache,
    cache_lengths,
    expert_ids,
    route_weights,
    w_gate,
    w_up,
    w_down,
):
    experts_all = lax.axis_size("expert")
    rows_dev = inputs.shape[1]
    per_group = HEADS // KV_HEADS
    capacity = max(2, 2 * rows_dev * TOPK // experts_all)
    shares = lax.axis_size("group")

    here = lax.axis_index("group")
    pair = 2 if shares % 2 == 0 else 1
    lines = shares // pair
    offsets = [(0, 1), (1, 0), (lines - 1, 0), (1, 1), (lines - 1, 1)]
    offsets += [(step, side) for step in range(2, lines - 1) for side in range(pair)]
    offsets = [o for o in dict.fromkeys(offsets) if o != (0, 0) and o[1] < pair]
    line, side_here = here // pair, here % pair
    sources = jnp.stack(
        [here] + [((line - dy) % lines) * pair + (side_here ^ dx) for dy, dx in offsets]
    ).astype(jnp.int32)

    def gather_shares(weight):
        received = [weight[0]]
        for dy, dx in offsets:
            pairs = [
                (i, ((i // pair + dy) % lines) * pair + ((i % pair) ^ dx)) for i in range(shares)
            ]
            received.append(lax.ppermute(weight[0], "group", pairs))
        return jnp.stack(received)

    gate_stack = gather_shares(w_gate)
    up_stack = gather_shares(w_up)
    down_stack = gather_shares(w_down)
    key_rows = key_cache.reshape(rows_dev, CACHE, KV_HEADS, HEAD_DIM)
    value_rows = value_cache.reshape(rows_dev, CACHE, KV_HEADS, HEAD_DIM)
    cache_ok = jnp.arange(CACHE, dtype=jnp.int32)[None, :] < cache_lengths[:, None]
    slot_columns = jnp.arange(experts_all * capacity, dtype=jnp.int32)
    expert_range = jnp.arange(experts_all, dtype=jnp.int32)
    results = []
    for step_index in range(STEPS):
        fresh = step_index + 1
        fresh_keys = jnp.swapaxes(new_keys[:fresh], 0, 1).reshape(
            rows_dev, fresh, KV_HEADS, HEAD_DIM
        )
        fresh_values = jnp.swapaxes(new_values[:fresh], 0, 1).reshape(
            rows_dev, fresh, KV_HEADS, HEAD_DIM
        )
        query_vals = queries[step_index].reshape(rows_dev, KV_HEADS, per_group, HEAD_DIM)
        attended = attend_rows(query_vals, key_rows, value_rows, cache_ok, fresh_keys, fresh_values)
        hidden = (inputs[step_index].astype(jnp.float32) + attended.reshape(rows_dev, -1)).astype(
            jnp.bfloat16
        )
        chosen = expert_ids[step_index].reshape(-1)
        onehot = (chosen[:, None] == expert_range[None, :]).astype(jnp.int32)
        before = jnp.cumsum(onehot, axis=0) - onehot
        slot_rank = jnp.sum(before * onehot, axis=1)
        target = chosen * capacity + slot_rank
        placed = (target[:, None] == slot_columns[None, :]).reshape(rows_dev, TOPK, -1)
        spread = jnp.any(placed, axis=1).astype(jnp.bfloat16)
        outgoing = jnp.einsum(
            "rc,rd->cd", spread, hidden, preferred_element_type=jnp.float32
        ).astype(jnp.bfloat16)
        outgoing = outgoing.reshape(experts_all, capacity, -1)
        mixing = jnp.sum(jnp.where(placed, route_weights[step_index][:, :, None], 0.0), axis=1)
        arrived = lax.all_to_all(outgoing, "expert", split_axis=0, concat_axis=0, tiled=True)
        num_slots, item_count, feature_dim = arrived.shape
        tokens = arrived.reshape(num_slots * item_count, feature_dim)
        expert_out = expert_ffn(sources, tokens, gate_stack, up_stack, down_stack)
        returned = lax.all_to_all(
            expert_out.reshape(num_slots, item_count, feature_dim),
            "expert",
            split_axis=0,
            concat_axis=0,
            tiled=True,
        )
        combined = jnp.dot(
            mixing,
            returned.reshape(experts_all * capacity, -1).astype(jnp.float32),
            precision=lax.Precision.HIGHEST,
        )
        results.append((hidden.astype(jnp.float32) + combined).astype(jnp.bfloat16))
    return jnp.stack(results)


def solution(mesh):
    in_specs = (
        P(None, ("group", "expert"), None),
        P(None, ("group", "expert"), None),
        P(None, ("group", "expert"), None),
        P(None, ("group", "expert"), None),
        P(("group", "expert"), None, None),
        P(("group", "expert"), None, None),
        P(("group", "expert")),
        P(None, ("group", "expert"), None),
        P(None, ("group", "expert"), None),
        P("expert", "group", None),
        P("expert", "group", None),
        P("expert", None, "group"),
    )
    out_specs = P(None, ("group", "expert"), None)
    return jax.shard_map(shards, mesh=mesh, in_specs=in_specs, out_specs=out_specs, check_vma=False)
```

```python
import jax
import jax.numpy as jnp
from jax import lax
from jax.experimental import pallas as pl
from jax.experimental.pallas import tpu as pltpu
from jax.sharding import PartitionSpec as P

HEADS = 32
KV_HEADS = 2
HEAD_DIM = 64
TOPK = 8
CACHE = 384
STEPS = 3


def attend_rows(query_vals, key_rows, value_rows, cache_ok, fresh_keys, fresh_values):
    factor = HEAD_DIM ** (-0.5)
    old_scores = (
        jnp.einsum("bkgd,bjkd->bkgj", query_vals, key_rows, preferred_element_type=jnp.float32)
        * factor
    )
    old_scores = jnp.where(cache_ok[:, None, None, :], old_scores, -1e30)
    new_scores = (
        jnp.einsum("bkgd,bjkd->bkgj", query_vals, fresh_keys, preferred_element_type=jnp.float32)
        * factor
    )
    highest = jnp.maximum(
        jnp.max(old_scores, axis=-1, keepdims=True), jnp.max(new_scores, axis=-1, keepdims=True)
    )
    old_weights = jnp.exp(old_scores - highest)
    new_weights = jnp.exp(new_scores - highest)
    denom_sum = jnp.sum(old_weights, axis=-1, keepdims=True) + jnp.sum(
        new_weights, axis=-1, keepdims=True
    )
    old_probs = (old_weights / denom_sum).astype(jnp.bfloat16)
    new_probs = (new_weights / denom_sum).astype(jnp.bfloat16)
    attended = jnp.einsum(
        "bkgj,bjkd->bkgd", old_probs, value_rows, preferred_element_type=jnp.float32
    )
    return attended + jnp.einsum(
        "bkgj,bjkd->bkgd", new_probs, fresh_values, preferred_element_type=jnp.float32
    )


def expert_ffn(here, tokens, paired_stack, down_stack):
    shares, _, block, hidden_units = paired_stack.shape
    slots, width = tokens.shape
    token_blocks = tokens.reshape(slots, shares, block).transpose(1, 0, 2)

    def kernel(here_ref, tok_ref, paired_ref, down_ref, out_ref):
        origin = here_ref[0]
        gate = up = None
        for k in range(shares):
            piece = tok_ref[(origin - k + shares) % shares]
            g = jnp.dot(piece, paired_ref[k, 0], preferred_element_type=jnp.float32)
            u = jnp.dot(piece, paired_ref[k, 1], preferred_element_type=jnp.float32)
            gate = g if gate is None else gate + g
            up = u if up is None else up + u
        activated = (gate / (1.0 + jnp.exp(-gate)) * up).astype(jnp.bfloat16)
        for k in range(shares):
            out_ref[(origin - k + shares) % shares] = jnp.dot(
                activated, down_ref[k], preferred_element_type=jnp.float32
            ).astype(out_ref.dtype)

    vmem = pl.BlockSpec(memory_space=pltpu.VMEM)
    out = pl.pallas_call(
        kernel,
        out_shape=jax.ShapeDtypeStruct((shares, slots, block), jnp.bfloat16),
        in_specs=[pl.BlockSpec(memory_space=pltpu.SMEM)] + [vmem] * 3,
        out_specs=vmem,
        cost_estimate=pl.CostEstimate(
            flops=6 * slots * width * hidden_units,
            transcendentals=slots * hidden_units,
            bytes_accessed=2 * (3 * width * hidden_units + 2 * slots * width),
        ),
    )(jnp.reshape(here, (1,)).astype(jnp.int32), token_blocks, paired_stack, down_stack)
    return out.transpose(1, 0, 2).reshape(slots, width)


def shards(
    inputs,
    queries,
    new_keys,
    new_values,
    key_cache,
    value_cache,
    cache_lengths,
    expert_ids,
    route_weights,
    w_gate,
    w_up,
    w_down,
):
    experts_all = lax.axis_size("expert")
    rows_dev = inputs.shape[1]
    per_group = HEADS // KV_HEADS
    capacity = max(2, 2 * rows_dev * TOPK // experts_all)
    shares = lax.axis_size("group")

    here = lax.axis_index("group")

    def gather_shares(share):
        received = [share]
        for shift in range(1, shares):
            pairs = [(i, (i + shift) % shares) for i in range(shares)]
            received.append(lax.ppermute(share, "group", pairs))
        return jnp.stack(received)

    paired_stack = gather_shares(jnp.concatenate([w_gate, w_up]))
    down_stack = gather_shares(w_down[0])
    key_rows = key_cache.reshape(rows_dev, CACHE, KV_HEADS, HEAD_DIM)
    value_rows = value_cache.reshape(rows_dev, CACHE, KV_HEADS, HEAD_DIM)
    cache_ok = jnp.arange(CACHE, dtype=jnp.int32)[None, :] < cache_lengths[:, None]
    slot_columns = jnp.arange(experts_all * capacity, dtype=jnp.int32)
    expert_range = jnp.arange(experts_all, dtype=jnp.int32)
    results = []
    for step_index in range(STEPS):
        fresh = step_index + 1
        fresh_keys = jnp.swapaxes(new_keys[:fresh], 0, 1).reshape(
            rows_dev, fresh, KV_HEADS, HEAD_DIM
        )
        fresh_values = jnp.swapaxes(new_values[:fresh], 0, 1).reshape(
            rows_dev, fresh, KV_HEADS, HEAD_DIM
        )
        query_vals = queries[step_index].reshape(rows_dev, KV_HEADS, per_group, HEAD_DIM)
        attended = attend_rows(query_vals, key_rows, value_rows, cache_ok, fresh_keys, fresh_values)
        hidden = (inputs[step_index].astype(jnp.float32) + attended.reshape(rows_dev, -1)).astype(
            jnp.bfloat16
        )
        chosen = expert_ids[step_index].reshape(-1)
        onehot = (chosen[:, None] == expert_range[None, :]).astype(jnp.int32)
        before = jnp.cumsum(onehot, axis=0) - onehot
        slot_rank = jnp.sum(before * onehot, axis=1)
        target = chosen * capacity + slot_rank
        placed = (target[:, None] == slot_columns[None, :]).reshape(rows_dev, TOPK, -1)
        spread = jnp.any(placed, axis=1).astype(jnp.bfloat16)
        outgoing = jnp.einsum(
            "rc,rd->cd", spread, hidden, preferred_element_type=jnp.float32
        ).astype(jnp.bfloat16)
        outgoing = outgoing.reshape(experts_all, capacity, -1)
        mixing = jnp.sum(jnp.where(placed, route_weights[step_index][:, :, None], 0.0), axis=1)
        arrived = lax.all_to_all(outgoing, "expert", split_axis=0, concat_axis=0, tiled=True)
        num_slots, item_count, feature_dim = arrived.shape
        tokens = arrived.reshape(num_slots * item_count, feature_dim)
        expert_out = expert_ffn(here, tokens, paired_stack, down_stack)
        returned = lax.all_to_all(
            expert_out.reshape(num_slots, item_count, feature_dim),
            "expert",
            split_axis=0,
            concat_axis=0,
            tiled=True,
        )
        combined = jnp.dot(
            mixing,
            returned.reshape(experts_all * capacity, -1).astype(jnp.float32),
            precision=lax.Precision.HIGHEST,
        )
        results.append((hidden.astype(jnp.float32) + combined).astype(jnp.bfloat16))
    return jnp.stack(results)


def solution(mesh):
    in_specs = (
        P(None, ("group", "expert"), None),
        P(None, ("group", "expert"), None),
        P(None, ("group", "expert"), None),
        P(None, ("group", "expert"), None),
        P(("group", "expert"), None, None),
        P(("group", "expert"), None, None),
        P(("group", "expert")),
        P(None, ("group", "expert"), None),
        P(None, ("group", "expert"), None),
        P("expert", "group", None),
        P("expert", "group", None),
        P("expert", None, "group"),
    )
    out_specs = P(None, ("group", "expert"), None)
    return jax.shard_map(shards, mesh=mesh, in_specs=in_specs, out_specs=out_specs, check_vma=False)
```

```python
import jax
import jax.numpy as jnp
from jax import lax
from jax.experimental import pallas as pl
from jax.experimental.pallas import tpu as pltpu
from jax.sharding import PartitionSpec as P

HEADS = 32
KV_HEADS = 2
HEAD_DIM = 64
TOPK = 8
CACHE = 384
STEPS = 3


def attend_rows(query_vals, key_rows, value_rows, cache_ok, fresh_keys, fresh_values):
    factor = HEAD_DIM ** (-0.5)
    old_scores = (
        jnp.einsum("bkgd,bjkd->bkgj", query_vals, key_rows, preferred_element_type=jnp.float32)
        * factor
    )
    old_scores = jnp.where(cache_ok[:, None, None, :], old_scores, -1e30)
    new_scores = (
        jnp.einsum("bkgd,bjkd->bkgj", query_vals, fresh_keys, preferred_element_type=jnp.float32)
        * factor
    )
    highest = jnp.maximum(
        jnp.max(old_scores, axis=-1, keepdims=True), jnp.max(new_scores, axis=-1, keepdims=True)
    )
    old_weights = jnp.exp(old_scores - highest)
    new_weights = jnp.exp(new_scores - highest)
    denom_sum = jnp.sum(old_weights, axis=-1, keepdims=True) + jnp.sum(
        new_weights, axis=-1, keepdims=True
    )
    old_probs = (old_weights / denom_sum).astype(jnp.bfloat16)
    new_probs = (new_weights / denom_sum).astype(jnp.bfloat16)
    attended = jnp.einsum(
        "bkgj,bjkd->bkgd", old_probs, value_rows, preferred_element_type=jnp.float32
    )
    return attended + jnp.einsum(
        "bkgj,bjkd->bkgd", new_probs, fresh_values, preferred_element_type=jnp.float32
    )


def expert_ffn(here, tokens, gate_stack, up_stack, down_stack):
    shares, block, hidden_units = gate_stack.shape
    slots, width = tokens.shape
    token_blocks = tokens.reshape(slots, shares, block).transpose(1, 0, 2)

    def kernel(here_ref, tok_ref, gate_ref, up_ref, down_ref, out_ref):
        origin = here_ref[0]
        gate = up = None
        for k in range(shares):
            piece = tok_ref[(origin - k + shares) % shares]
            g = jnp.dot(piece, gate_ref[k], preferred_element_type=jnp.float32)
            u = jnp.dot(piece, up_ref[k], preferred_element_type=jnp.float32)
            gate = g if gate is None else gate + g
            up = u if up is None else up + u
        activated = (gate / (1.0 + jnp.exp(-gate)) * up).astype(jnp.bfloat16)
        for k in range(shares):
            out_ref[(origin - k + shares) % shares] = jnp.dot(
                activated, down_ref[k], preferred_element_type=jnp.float32
            ).astype(out_ref.dtype)

    vmem = pl.BlockSpec(memory_space=pltpu.VMEM)
    out = pl.pallas_call(
        kernel,
        out_shape=jax.ShapeDtypeStruct((shares, slots, block), jnp.bfloat16),
        in_specs=[pl.BlockSpec(memory_space=pltpu.SMEM)] + [vmem] * 4,
        out_specs=vmem,
        cost_estimate=pl.CostEstimate(
            flops=6 * slots * width * hidden_units,
            transcendentals=slots * hidden_units,
            bytes_accessed=2 * (3 * width * hidden_units + 2 * slots * width),
        ),
    )(jnp.reshape(here, (1,)).astype(jnp.int32), token_blocks, gate_stack, up_stack, down_stack)
    return out.transpose(1, 0, 2).reshape(slots, width)


def shards(
    inputs,
    queries,
    new_keys,
    new_values,
    key_cache,
    value_cache,
    cache_lengths,
    expert_ids,
    route_weights,
    w_gate,
    w_up,
    w_down,
):
    experts_all = lax.axis_size("expert")
    rows_dev = inputs.shape[1]
    per_group = HEADS // KV_HEADS
    capacity = max(2, 2 * rows_dev * TOPK // experts_all)
    shares = lax.axis_size("group")

    here = lax.axis_index("group")

    def gather_shares(weight):
        share = weight[0]
        halves = share.reshape((2, share.shape[0] // 2) + share.shape[1:])
        received = [halves]
        for shift in range(1, shares):
            pairs = [(i, (i + shift) % shares) for i in range(shares)]
            received.append(
                jnp.stack([lax.ppermute(halves[h], "group", pairs) for h in range(2)])
            )
        return jnp.stack(received).reshape((shares,) + share.shape)

    gate_stack = gather_shares(w_gate)
    up_stack = gather_shares(w_up)
    down_stack = gather_shares(w_down)
    key_rows = key_cache.reshape(rows_dev, CACHE, KV_HEADS, HEAD_DIM)
    value_rows = value_cache.reshape(rows_dev, CACHE, KV_HEADS, HEAD_DIM)
    cache_ok = jnp.arange(CACHE, dtype=jnp.int32)[None, :] < cache_lengths[:, None]
    slot_columns = jnp.arange(experts_all * capacity, dtype=jnp.int32)
    expert_range = jnp.arange(experts_all, dtype=jnp.int32)
    results = []
    for step_index in range(STEPS):
        fresh = step_index + 1
        fresh_keys = jnp.swapaxes(new_keys[:fresh], 0, 1).reshape(
            rows_dev, fresh, KV_HEADS, HEAD_DIM
        )
        fresh_values = jnp.swapaxes(new_values[:fresh], 0, 1).reshape(
            rows_dev, fresh, KV_HEADS, HEAD_DIM
        )
        query_vals = queries[step_index].reshape(rows_dev, KV_HEADS, per_group, HEAD_DIM)
        attended = attend_rows(query_vals, key_rows, value_rows, cache_ok, fresh_keys, fresh_values)
        hidden = (inputs[step_index].astype(jnp.float32) + attended.reshape(rows_dev, -1)).astype(
            jnp.bfloat16
        )
        chosen = expert_ids[step_index].reshape(-1)
        onehot = (chosen[:, None] == expert_range[None, :]).astype(jnp.int32)
        before = jnp.cumsum(onehot, axis=0) - onehot
        slot_rank = jnp.sum(before * onehot, axis=1)
        target = chosen * capacity + slot_rank
        placed = (target[:, None] == slot_columns[None, :]).reshape(rows_dev, TOPK, -1)
        spread = jnp.any(placed, axis=1).astype(jnp.bfloat16)
        outgoing = jnp.einsum(
            "rc,rd->cd", spread, hidden, preferred_element_type=jnp.float32
        ).astype(jnp.bfloat16)
        outgoing = outgoing.reshape(experts_all, capacity, -1)
        mixing = jnp.sum(jnp.where(placed, route_weights[step_index][:, :, None], 0.0), axis=1)
        arrived = lax.all_to_all(outgoing, "expert", split_axis=0, concat_axis=0, tiled=True)
        num_slots, item_count, feature_dim = arrived.shape
        tokens = arrived.reshape(num_slots * item_count, feature_dim)
        expert_out = expert_ffn(here, tokens, gate_stack, up_stack, down_stack)
        returned = lax.all_to_all(
            expert_out.reshape(num_slots, item_count, feature_dim),
            "expert",
            split_axis=0,
            concat_axis=0,
            tiled=True,
        )
        combined = jnp.dot(
            mixing,
            returned.reshape(experts_all * capacity, -1).astype(jnp.float32),
            precision=lax.Precision.HIGHEST,
        )
        results.append((hidden.astype(jnp.float32) + combined).astype(jnp.bfloat16))
    return jnp.stack(results)


def solution(mesh):
    in_specs = (
        P(None, ("group", "expert"), None),
        P(None, ("group", "expert"), None),
        P(None, ("group", "expert"), None),
        P(None, ("group", "expert"), None),
        P(("group", "expert"), None, None),
        P(("group", "expert"), None, None),
        P(("group", "expert")),
        P(None, ("group", "expert"), None),
        P(None, ("group", "expert"), None),
        P("expert", "group", None),
        P("expert", "group", None),
        P("expert", None, "group"),
    )
    out_specs = P(None, ("group", "expert"), None)
    return jax.shard_map(shards, mesh=mesh, in_specs=in_specs, out_specs=out_specs, check_vma=False)
```

```python
import jax
import jax.numpy as jnp
from jax import lax
from jax.experimental import pallas as pl
from jax.experimental.pallas import tpu as pltpu
from jax.sharding import PartitionSpec as P

HEADS = 32
KV_HEADS = 2
HEAD_DIM = 64
TOPK = 8
CACHE = 384
STEPS = 3


def attend_rows(query_vals, key_rows, value_rows, cache_ok, fresh_keys, fresh_values):
    factor = HEAD_DIM ** (-0.5)
    old_scores = (
        jnp.einsum("bkgd,bjkd->bkgj", query_vals, key_rows, preferred_element_type=jnp.float32)
        * factor
    )
    old_scores = jnp.where(cache_ok[:, None, None, :], old_scores, -1e30)
    new_scores = (
        jnp.einsum("bkgd,bjkd->bkgj", query_vals, fresh_keys, preferred_element_type=jnp.float32)
        * factor
    )
    highest = jnp.maximum(
        jnp.max(old_scores, axis=-1, keepdims=True), jnp.max(new_scores, axis=-1, keepdims=True)
    )
    old_weights = jnp.exp(old_scores - highest)
    new_weights = jnp.exp(new_scores - highest)
    denom_sum = jnp.sum(old_weights, axis=-1, keepdims=True) + jnp.sum(
        new_weights, axis=-1, keepdims=True
    )
    old_probs = (old_weights / denom_sum).astype(jnp.bfloat16)
    new_probs = (new_weights / denom_sum).astype(jnp.bfloat16)
    attended = jnp.einsum(
        "bkgj,bjkd->bkgd", old_probs, value_rows, preferred_element_type=jnp.float32
    )
    return attended + jnp.einsum(
        "bkgj,bjkd->bkgd", new_probs, fresh_values, preferred_element_type=jnp.float32
    )


def expert_ffn(here, tokens, gate_stack, up_stack, down_stack):
    shares, block, hidden_units = gate_stack.shape
    slots, width = tokens.shape

    def kernel(here_ref, tok_ref, gate_ref, up_ref, down_ref, out_ref):
        origin = here_ref[0]
        gate = up = None
        for j in range(shares):
            held = (origin - j + shares) % shares
            piece = tok_ref[:, j * block:(j + 1) * block]
            g = jnp.dot(piece, gate_ref[held], preferred_element_type=jnp.float32)
            u = jnp.dot(piece, up_ref[held], preferred_element_type=jnp.float32)
            gate = g if gate is None else gate + g
            up = u if up is None else up + u
        activated = (gate / (1.0 + jnp.exp(-gate)) * up).astype(jnp.bfloat16)
        for j in range(shares):
            held = (origin - j + shares) % shares
            out_ref[:, j * block:(j + 1) * block] = jnp.dot(
                activated, down_ref[held], preferred_element_type=jnp.float32
            ).astype(out_ref.dtype)

    vmem = pl.BlockSpec(memory_space=pltpu.VMEM)
    return pl.pallas_call(
        kernel,
        out_shape=jax.ShapeDtypeStruct((slots, width), jnp.bfloat16),
        in_specs=[pl.BlockSpec(memory_space=pltpu.SMEM)] + [vmem] * 4,
        out_specs=vmem,
        cost_estimate=pl.CostEstimate(
            flops=6 * slots * width * hidden_units,
            transcendentals=slots * hidden_units,
            bytes_accessed=2 * (3 * width * hidden_units + 2 * slots * width),
        ),
    )(jnp.reshape(here, (1,)).astype(jnp.int32), tokens, gate_stack, up_stack, down_stack)


def shards(
    inputs,
    queries,
    new_keys,
    new_values,
    key_cache,
    value_cache,
    cache_lengths,
    expert_ids,
    route_weights,
    w_gate,
    w_up,
    w_down,
):
    experts_all = lax.axis_size("expert")
    rows_dev = inputs.shape[1]
    per_group = HEADS // KV_HEADS
    capacity = max(2, 2 * rows_dev * TOPK // experts_all)
    shares = lax.axis_size("group")

    here = lax.axis_index("group")

    def gather_shares(weight):
        received = [weight[0]]
        for shift in range(1, shares):
            pairs = [(i, (i + shift) % shares) for i in range(shares)]
            received.append(lax.ppermute(weight[0], "group", pairs))
        return jnp.stack(received)

    gate_stack = gather_shares(w_gate)
    up_stack = gather_shares(w_up)
    down_stack = gather_shares(w_down)
    key_rows = key_cache.reshape(rows_dev, CACHE, KV_HEADS, HEAD_DIM)
    value_rows = value_cache.reshape(rows_dev, CACHE, KV_HEADS, HEAD_DIM)
    cache_ok = jnp.arange(CACHE, dtype=jnp.int32)[None, :] < cache_lengths[:, None]
    slot_columns = jnp.arange(experts_all * capacity, dtype=jnp.int32)
    expert_range = jnp.arange(experts_all, dtype=jnp.int32)
    results = []
    for step_index in range(STEPS):
        fresh = step_index + 1
        fresh_keys = jnp.swapaxes(new_keys[:fresh], 0, 1).reshape(
            rows_dev, fresh, KV_HEADS, HEAD_DIM
        )
        fresh_values = jnp.swapaxes(new_values[:fresh], 0, 1).reshape(
            rows_dev, fresh, KV_HEADS, HEAD_DIM
        )
        query_vals = queries[step_index].reshape(rows_dev, KV_HEADS, per_group, HEAD_DIM)
        attended = attend_rows(query_vals, key_rows, value_rows, cache_ok, fresh_keys, fresh_values)
        hidden = (inputs[step_index].astype(jnp.float32) + attended.reshape(rows_dev, -1)).astype(
            jnp.bfloat16
        )
        chosen = expert_ids[step_index].reshape(-1)
        onehot = (chosen[:, None] == expert_range[None, :]).astype(jnp.int32)
        before = jnp.cumsum(onehot, axis=0) - onehot
        slot_rank = jnp.sum(before * onehot, axis=1)
        target = chosen * capacity + slot_rank
        placed = (target[:, None] == slot_columns[None, :]).reshape(rows_dev, TOPK, -1)
        spread = jnp.any(placed, axis=1).astype(jnp.bfloat16)
        outgoing = jnp.einsum(
            "rc,rd->cd", spread, hidden, preferred_element_type=jnp.float32
        ).astype(jnp.bfloat16)
        outgoing = outgoing.reshape(experts_all, capacity, -1)
        mixing = jnp.sum(jnp.where(placed, route_weights[step_index][:, :, None], 0.0), axis=1)
        arrived = lax.all_to_all(outgoing, "expert", split_axis=0, concat_axis=0, tiled=True)
        num_slots, item_count, feature_dim = arrived.shape
        tokens = arrived.reshape(num_slots * item_count, feature_dim)
        expert_out = expert_ffn(here, tokens, gate_stack, up_stack, down_stack)
        returned = lax.all_to_all(
            expert_out.reshape(num_slots, item_count, feature_dim),
            "expert",
            split_axis=0,
            concat_axis=0,
            tiled=True,
        )
        combined = jnp.dot(
            mixing,
            returned.reshape(experts_all * capacity, -1).astype(jnp.float32),
            precision=lax.Precision.HIGHEST,
        )
        results.append((hidden.astype(jnp.float32) + combined).astype(jnp.bfloat16))
    return jnp.stack(results)


def solution(mesh):
    in_specs = (
        P(None, ("group", "expert"), None),
        P(None, ("group", "expert"), None),
        P(None, ("group", "expert"), None),
        P(None, ("group", "expert"), None),
        P(("group", "expert"), None, None),
        P(("group", "expert"), None, None),
        P(("group", "expert")),
        P(None, ("group", "expert"), None),
        P(None, ("group", "expert"), None),
        P("expert", "group", None),
        P("expert", "group", None),
        P("expert", None, "group"),
    )
    out_specs = P(None, ("group", "expert"), None)
    return jax.shard_map(shards, mesh=mesh, in_specs=in_specs, out_specs=out_specs, check_vma=False)
```

```python
import jax
import jax.numpy as jnp
from jax import lax
from jax.experimental import pallas as pl
from jax.experimental.pallas import tpu as pltpu
from jax.sharding import PartitionSpec as P

HEADS = 32
KV_HEADS = 2
HEAD_DIM = 64
TOPK = 8
CACHE = 384
STEPS = 3


def attend_rows(query_vals, key_rows, value_rows, cache_ok, fresh_keys, fresh_values):
    factor = HEAD_DIM ** (-0.5)
    old_scores = (
        jnp.einsum("bkgd,bjkd->bkgj", query_vals, key_rows, preferred_element_type=jnp.float32)
        * factor
    )
    old_scores = jnp.where(cache_ok[:, None, None, :], old_scores, -1e30)
    new_scores = (
        jnp.einsum("bkgd,bjkd->bkgj", query_vals, fresh_keys, preferred_element_type=jnp.float32)
        * factor
    )
    highest = jnp.maximum(
        jnp.max(old_scores, axis=-1, keepdims=True), jnp.max(new_scores, axis=-1, keepdims=True)
    )
    old_weights = jnp.exp(old_scores - highest)
    new_weights = jnp.exp(new_scores - highest)
    denom_sum = jnp.sum(old_weights, axis=-1, keepdims=True) + jnp.sum(
        new_weights, axis=-1, keepdims=True
    )
    old_probs = (old_weights / denom_sum).astype(jnp.bfloat16)
    new_probs = (new_weights / denom_sum).astype(jnp.bfloat16)
    attended = jnp.einsum(
        "bkgj,bjkd->bkgd", old_probs, value_rows, preferred_element_type=jnp.float32
    )
    return attended + jnp.einsum(
        "bkgj,bjkd->bkgd", new_probs, fresh_values, preferred_element_type=jnp.float32
    )


def expert_ffn(here, tokens, gate_stack, up_stack, down_stack):
    shares, block, hidden_units = gate_stack.shape
    rows, per_row, width = tokens.shape
    slots = rows * per_row

    def kernel(here_ref, tok_ref, gate_ref, up_ref, down_ref, out_ref):
        origin = here_ref[0]
        gate = up = None
        for j in range(shares):
            held = (origin - j + shares) % shares
            piece = tok_ref[:, :, j * block:(j + 1) * block].reshape(slots, block)
            g = jnp.dot(piece, gate_ref[held], preferred_element_type=jnp.float32)
            u = jnp.dot(piece, up_ref[held], preferred_element_type=jnp.float32)
            gate = g if gate is None else gate + g
            up = u if up is None else up + u
        activated = (gate / (1.0 + jnp.exp(-gate)) * up).astype(jnp.bfloat16)
        for j in range(shares):
            held = (origin - j + shares) % shares
            out_ref[:, :, j * block:(j + 1) * block] = (
                jnp.dot(activated, down_ref[held], preferred_element_type=jnp.float32)
                .astype(out_ref.dtype)
                .reshape(rows, per_row, block)
            )

    vmem = pl.BlockSpec(memory_space=pltpu.VMEM)
    return pl.pallas_call(
        kernel,
        out_shape=jax.ShapeDtypeStruct((rows, per_row, width), jnp.bfloat16),
        in_specs=[pl.BlockSpec(memory_space=pltpu.SMEM)] + [vmem] * 4,
        out_specs=vmem,
        cost_estimate=pl.CostEstimate(
            flops=6 * slots * width * hidden_units,
            transcendentals=slots * hidden_units,
            bytes_accessed=2 * (3 * width * hidden_units + 2 * slots * width),
        ),
    )(jnp.reshape(here, (1,)).astype(jnp.int32), tokens, gate_stack, up_stack, down_stack)


def shards(
    inputs,
    queries,
    new_keys,
    new_values,
    key_cache,
    value_cache,
    cache_lengths,
    expert_ids,
    route_weights,
    w_gate,
    w_up,
    w_down,
):
    experts_all = lax.axis_size("expert")
    rows_dev = inputs.shape[1]
    per_group = HEADS // KV_HEADS
    capacity = max(2, 2 * rows_dev * TOPK // experts_all)
    shares = lax.axis_size("group")

    here = lax.axis_index("group")

    def gather_shares(weight):
        received = [weight[0]]
        for shift in range(1, shares):
            pairs = [(i, (i + shift) % shares) for i in range(shares)]
            received.append(lax.ppermute(weight[0], "group", pairs))
        return jnp.stack(received)

    gate_stack = gather_shares(w_gate)
    up_stack = gather_shares(w_up)
    down_stack = gather_shares(w_down)
    key_rows = key_cache.reshape(rows_dev, CACHE, KV_HEADS, HEAD_DIM)
    value_rows = value_cache.reshape(rows_dev, CACHE, KV_HEADS, HEAD_DIM)
    cache_ok = jnp.arange(CACHE, dtype=jnp.int32)[None, :] < cache_lengths[:, None]
    slot_columns = jnp.arange(experts_all * capacity, dtype=jnp.int32)
    expert_range = jnp.arange(experts_all, dtype=jnp.int32)
    results = []
    for step_index in range(STEPS):
        fresh = step_index + 1
        fresh_keys = jnp.swapaxes(new_keys[:fresh], 0, 1).reshape(
            rows_dev, fresh, KV_HEADS, HEAD_DIM
        )
        fresh_values = jnp.swapaxes(new_values[:fresh], 0, 1).reshape(
            rows_dev, fresh, KV_HEADS, HEAD_DIM
        )
        query_vals = queries[step_index].reshape(rows_dev, KV_HEADS, per_group, HEAD_DIM)
        attended = attend_rows(query_vals, key_rows, value_rows, cache_ok, fresh_keys, fresh_values)
        hidden = (inputs[step_index].astype(jnp.float32) + attended.reshape(rows_dev, -1)).astype(
            jnp.bfloat16
        )
        chosen = expert_ids[step_index].reshape(-1)
        onehot = (chosen[:, None] == expert_range[None, :]).astype(jnp.int32)
        before = jnp.cumsum(onehot, axis=0) - onehot
        slot_rank = jnp.sum(before * onehot, axis=1)
        target = chosen * capacity + slot_rank
        placed = (target[:, None] == slot_columns[None, :]).reshape(rows_dev, TOPK, -1)
        spread = jnp.any(placed, axis=1).astype(jnp.bfloat16)
        outgoing = jnp.einsum(
            "rc,rd->cd", spread, hidden, preferred_element_type=jnp.float32
        ).astype(jnp.bfloat16)
        outgoing = outgoing.reshape(experts_all, capacity, -1)
        mixing = jnp.sum(jnp.where(placed, route_weights[step_index][:, :, None], 0.0), axis=1)
        arrived = lax.all_to_all(outgoing, "expert", split_axis=0, concat_axis=0, tiled=True)
        tokens = arrived
        expert_out = expert_ffn(here, tokens, gate_stack, up_stack, down_stack)
        returned = lax.all_to_all(
            expert_out,
            "expert",
            split_axis=0,
            concat_axis=0,
            tiled=True,
        )
        combined = jnp.dot(
            mixing,
            returned.reshape(experts_all * capacity, -1).astype(jnp.float32),
            precision=lax.Precision.HIGHEST,
        )
        results.append((hidden.astype(jnp.float32) + combined).astype(jnp.bfloat16))
    return jnp.stack(results)


def solution(mesh):
    in_specs = (
        P(None, ("group", "expert"), None),
        P(None, ("group", "expert"), None),
        P(None, ("group", "expert"), None),
        P(None, ("group", "expert"), None),
        P(("group", "expert"), None, None),
        P(("group", "expert"), None, None),
        P(("group", "expert")),
        P(None, ("group", "expert"), None),
        P(None, ("group", "expert"), None),
        P("expert", "group", None),
        P("expert", "group", None),
        P("expert", None, "group"),
    )
    out_specs = P(None, ("group", "expert"), None)
    return jax.shard_map(shards, mesh=mesh, in_specs=in_specs, out_specs=out_specs, check_vma=False)
```

```python
import jax
import jax.numpy as jnp
from jax import lax
from jax.experimental import pallas as pl
from jax.experimental.pallas import tpu as pltpu
from jax.sharding import PartitionSpec as P

HEADS = 32
KV_HEADS = 2
HEAD_DIM = 64
TOPK = 8
CACHE = 384
STEPS = 3


def attend_rows(query_vals, key_rows, value_rows, cache_ok, fresh_keys, fresh_values):
    factor = HEAD_DIM ** (-0.5)
    old_scores = (
        jnp.einsum("bkgd,bjkd->bkgj", query_vals, key_rows, preferred_element_type=jnp.float32)
        * factor
    )
    old_scores = jnp.where(cache_ok[:, None, None, :], old_scores, -1e30)
    new_scores = (
        jnp.einsum("bkgd,bjkd->bkgj", query_vals, fresh_keys, preferred_element_type=jnp.float32)
        * factor
    )
    highest = jnp.maximum(
        jnp.max(old_scores, axis=-1, keepdims=True), jnp.max(new_scores, axis=-1, keepdims=True)
    )
    old_weights = jnp.exp(old_scores - highest)
    new_weights = jnp.exp(new_scores - highest)
    denom_sum = jnp.sum(old_weights, axis=-1, keepdims=True) + jnp.sum(
        new_weights, axis=-1, keepdims=True
    )
    old_probs = (old_weights / denom_sum).astype(jnp.bfloat16)
    new_probs = (new_weights / denom_sum).astype(jnp.bfloat16)
    attended = jnp.einsum(
        "bkgj,bjkd->bkgd", old_probs, value_rows, preferred_element_type=jnp.float32
    )
    return attended + jnp.einsum(
        "bkgj,bjkd->bkgd", new_probs, fresh_values, preferred_element_type=jnp.float32
    )


def expert_ffn(here, tokens, gate_stack, up_stack, down_stack):
    shares, block, hidden_units = gate_stack.shape
    rows, per_row, width = tokens.shape
    slots = rows * per_row

    def kernel(here_ref, tok_ref, gate_ref, up_ref, down_ref, out_ref):
        origin = here_ref[0]
        gate = up = None
        for j in range(shares):
            held = (origin - j + shares) % shares
            piece = tok_ref[:, :, j * block:(j + 1) * block].reshape(slots, block)
            g = jnp.dot(piece, gate_ref[held], preferred_element_type=jnp.float32)
            u = jnp.dot(piece, up_ref[held], preferred_element_type=jnp.float32)
            gate = g if gate is None else gate + g
            up = u if up is None else up + u
        activated = (gate / (1.0 + jnp.exp(-gate)) * up).astype(jnp.bfloat16)
        for j in range(shares):
            held = (origin - j + shares) % shares
            out_ref[:, :, j * block:(j + 1) * block] = (
                jnp.dot(activated, down_ref[held], preferred_element_type=jnp.float32)
                .astype(out_ref.dtype)
                .reshape(rows, per_row, block)
            )

    vmem = pl.BlockSpec(memory_space=pltpu.VMEM)
    return pl.pallas_call(
        kernel,
        out_shape=jax.ShapeDtypeStruct((rows, per_row, width), jnp.bfloat16),
        in_specs=[pl.BlockSpec(memory_space=pltpu.SMEM)] + [vmem] * 4,
        out_specs=vmem,
        cost_estimate=pl.CostEstimate(
            flops=6 * slots * width * hidden_units,
            transcendentals=slots * hidden_units,
            bytes_accessed=2 * (3 * width * hidden_units + 2 * slots * width),
        ),
    )(jnp.reshape(here, (1,)).astype(jnp.int32), tokens, gate_stack, up_stack, down_stack)


def shards(
    inputs,
    queries,
    new_keys,
    new_values,
    key_cache,
    value_cache,
    cache_lengths,
    expert_ids,
    route_weights,
    w_gate,
    w_up,
    w_down,
):
    experts_all = lax.axis_size("expert")
    rows_dev = inputs.shape[1]
    per_group = HEADS // KV_HEADS
    capacity = max(2, 2 * rows_dev * TOPK // experts_all)
    shares = lax.axis_size("group")

    here = lax.axis_index("group")

    def gather_shares(weight):
        received = [weight[0]]
        for shift in range(1, shares):
            pairs = [(i, (i + shift) % shares) for i in range(shares)]
            received.append(lax.ppermute(weight[0], "group", pairs))
        return jnp.stack(received)

    gate_stack = gather_shares(w_gate)
    up_stack = gather_shares(w_up)
    down_stack = gather_shares(w_down)
    key_rows = key_cache.reshape(rows_dev, CACHE, KV_HEADS, HEAD_DIM)
    value_rows = value_cache.reshape(rows_dev, CACHE, KV_HEADS, HEAD_DIM)
    cache_ok = jnp.arange(CACHE, dtype=jnp.int32)[None, :] < cache_lengths[:, None]
    slot_columns = jnp.arange(experts_all * capacity, dtype=jnp.int32)
    expert_range = jnp.arange(experts_all, dtype=jnp.int32)
    results = []
    for step_index in range(STEPS):
        fresh = step_index + 1
        fresh_keys = jnp.swapaxes(new_keys[:fresh], 0, 1).reshape(
            rows_dev, fresh, KV_HEADS, HEAD_DIM
        )
        fresh_values = jnp.swapaxes(new_values[:fresh], 0, 1).reshape(
            rows_dev, fresh, KV_HEADS, HEAD_DIM
        )
        query_vals = queries[step_index].reshape(rows_dev, KV_HEADS, per_group, HEAD_DIM)
        attended = attend_rows(query_vals, key_rows, value_rows, cache_ok, fresh_keys, fresh_values)
        hidden = (inputs[step_index].astype(jnp.float32) + attended.reshape(rows_dev, -1)).astype(
            jnp.bfloat16
        )
        chosen = expert_ids[step_index].reshape(-1)
        onehot = (chosen[:, None] == expert_range[None, :]).astype(jnp.int32)
        before = jnp.cumsum(onehot, axis=0) - onehot
        slot_rank = jnp.sum(before * onehot, axis=1)
        target = chosen * capacity + slot_rank
        placed = (target[:, None] == slot_columns[None, :]).reshape(rows_dev, TOPK, -1)
        spread = jnp.any(placed, axis=1).astype(jnp.bfloat16)
        outgoing = jnp.einsum(
            "rec,rd->ecd",
            spread.reshape(rows_dev, experts_all, capacity),
            hidden,
            preferred_element_type=jnp.float32,
        ).astype(jnp.bfloat16)
        mixing = jnp.sum(jnp.where(placed, route_weights[step_index][:, :, None], 0.0), axis=1)
        arrived = lax.all_to_all(outgoing, "expert", split_axis=0, concat_axis=0, tiled=True)
        tokens = arrived
        expert_out = expert_ffn(here, tokens, gate_stack, up_stack, down_stack)
        returned = lax.all_to_all(
            expert_out,
            "expert",
            split_axis=0,
            concat_axis=0,
            tiled=True,
        )
        combined = jnp.einsum(
            "rec,ecd->rd",
            mixing.reshape(rows_dev, experts_all, capacity),
            returned.astype(jnp.float32),
            precision=lax.Precision.HIGHEST,
        )
        results.append((hidden.astype(jnp.float32) + combined).astype(jnp.bfloat16))
    return jnp.stack(results)


def solution(mesh):
    in_specs = (
        P(None, ("group", "expert"), None),
        P(None, ("group", "expert"), None),
        P(None, ("group", "expert"), None),
        P(None, ("group", "expert"), None),
        P(("group", "expert"), None, None),
        P(("group", "expert"), None, None),
        P(("group", "expert")),
        P(None, ("group", "expert"), None),
        P(None, ("group", "expert"), None),
        P("expert", "group", None),
        P("expert", "group", None),
        P("expert", None, "group"),
    )
    out_specs = P(None, ("group", "expert"), None)
    return jax.shard_map(shards, mesh=mesh, in_specs=in_specs, out_specs=out_specs, check_vma=False)
```
